32 devices in a mesh: plane: 4 (over y, x), tile: 8 (over z, core).
Axes of the slice: x: 2, y: 2, z: 4, core: 2. Of those that a mesh axis runs over, the one named last changes fastest.
Arguments:
- recording: bfloat16 [4, 8, 3, 4, 256, 128], P('plane', 'tile'), may hold values from -8 to 8
- start_vectors: float32 [4, 16, 32, 128], P('plane', 'tile'), may hold values from -5 to 5
- footprints: bfloat16 [4, 1024, 256], P('plane', 'tile'), may hold values from 0.00019931793 to 0.029907227
- source_row: int32 [4, 1024, 1], P('plane', 'tile'), may hold values from 0 to 5; in each aligned block of 128 rows (0 to 127, 128 to 255, ..., all dimensions but the last counted through in order) at most 32 rows name the same one
- footprint_block: int32 [4, 1024], P('plane', 'tile'), may hold values from 0 to 3
Outputs:
- temporal_factors: float32 [4, 16, 32, 128], P('plane', 'tile')
- traces: float32 [4, 1024, 128], P('plane', 'tile')
The draws below stay inside these ranges and needn't reach their ends.
Inputs may be any that keep to these rules, and one draw needn't show every extreme that they name: `source_row`: among the 128 sources of one device at most 32 share a value, and some value is shared by exactly 32 of them.
All inputs are finite; a program needn't handle non-finite values.
Results may differ from the reference program's by a relative error of at most 0.0069.
Values may be sent and summed in bfloat16 or wider, within the bound.
No kernel may reach another device: no remote copies, remote signals or barrier semaphores. Data moves between devices by JAX's collectives and lax.ppermute only.
A program may use at most 64 MiB of HBM per device.

```python
import math
import jax
import jax.numpy as jnp
import numpy as np
from jax import lax

BLK = 256
RANK = 32
FRAMES = 128
ITERS = 3
P_DEV = 2
SRC_DEV = 128
PLANES = 4
TILES = 8
CELLS = 3
PATCHES = 16
SRC = 1024
MOST = 32
N_TILE = 8


def draw_recording(key, part):
    key_noise, key_signal, key_gain = jax.random.split(key, 3)
    full_shape = (PLANES, TILES, CELLS, 4, BLK, FRAMES)
    noise_field = jnp.clip(jax.random.normal(key_noise, full_shape, jnp.float32), -5.0, 5.0)
    signal = jnp.clip(jax.random.normal(key_signal, (FRAMES,), jnp.float32), -4.0, 4.0)
    strip_ramp = 0.5 + 1.5 * jnp.arange(TILES, dtype=jnp.float32) / max(TILES - 1, 1)
    block_gain = jnp.exp(jax.random.uniform(key_gain, (PLANES, TILES, CELLS, 4, 1, 1), jnp.float32, 0.0, math.log(2.0)))
    plane_gain = 1.0 + 0.25 * jnp.arange(PLANES, dtype=jnp.float32)
    brightness = plane_gain[:, None, None, None, None, None] * strip_ramp[None, :, None, None, None, None] * block_gain
    return (noise_field + 0.1 * brightness * signal).astype(jnp.bfloat16)


def touch_ends(array, stream_key, low, top_value):
    place = [jax.random.randint(jax.random.fold_in(stream_key, axis), (), 0, length) for axis, length in enumerate(array.shape)]
    longest = array.shape.index(max(array.shape))
    neighbour = place[:longest] + [(place[longest] + 1) % array.shape[longest]] + place[longest + 1:]
    return array.at[tuple(place)].set(low).at[tuple(neighbour)].set(top_value)


def shard_levels(key, shape, cuts, least, largest):
    def one(position, parts):
        draws = jax.random.uniform(jax.random.fold_in(jax.random.fold_in(key, 6), position), (parts,), jnp.float32, least / len(cuts), largest / len(cuts))
        return jnp.repeat(jnp.exp(draws), shape[position] // parts).reshape((-1,) + (1,) * (len(shape) - position - 1))

    loudness = one(*cuts[0])
    for cut in cuts[1:]:
        loudness = loudness * one(*cut)
    return loudness


def routed_block(key, own, number, rows, amount, top, most, slope):
    sequence = jax.random.permutation(key, amount)
    packed, ordinary = shares(amount, rows * top, most, slope, True), shares(amount, rows * top, most, slope, False)
    places = jnp.arange(amount)

    def named(sizes, rotation):
        used = int((sizes > 0).sum())
        fixed = max(1, used // 4)
        passed = fixed + (places - fixed + rotation * (used - fixed)) % max(1, amount - fixed)
        return jnp.zeros((amount,), jnp.int32).at[sequence[jnp.where(places < fixed, places, passed)]].set(jnp.asarray(sizes, jnp.int32))

    sizes = jnp.where(number % 4 == 0, named(packed, number // 4), named(ordinary, number - number // 4 - 1))
    mixed = jax.random.permutation(jax.random.fold_in(own, 3), amount)
    giver, receiver = mixed[0:amount // 2 * 2:2], mixed[1:amount // 2 * 2:2]
    room = jnp.minimum(sizes[giver] - 1, most - sizes[receiver]) // 2
    room = jnp.where((giver == sequence[0]) | (receiver == sequence[0]) | (sizes[receiver] == 0), 0, jnp.maximum(room, 0))
    passed = jax.random.randint(jax.random.fold_in(own, 4), (amount // 2,), 0, 1 << 20) % (room + 1)
    sizes = sizes.at[giver].add(-passed).at[receiver].add(passed)
    labels = jnp.searchsorted(jnp.cumsum(sizes), jnp.arange(rows * top), side="right").astype(jnp.int32)
    listing = labels.reshape(top, rows).T
    listing = listing[jax.random.permutation(jax.random.fold_in(own, 1), rows)]
    rotation = jax.random.randint(jax.random.fold_in(own, 2), (rows, 1), 0, top)
    return jnp.take_along_axis(listing, (jnp.arange(top)[None, :] + rotation) % top, axis=1)


def shares(amount, total, limit, lean, full):
    portions = [(1 << 20) // math.isqrt(standing ** lean) + 1 for standing in range(1, amount + 1)]
    largest = limit if full else min(limit, max(-(-total // amount), total * portions[0] // sum(portions)))
    least = 1 if total - largest >= amount - 1 else 0
    holding, rest = [largest] + [least] * (amount - 1), total - largest - least * (amount - 1)
    while rest > 0:
        free = [i for i in range(1, amount) if holding[i] < largest] or [i for i in range(1, amount) if holding[i] < limit]
        mass, left = sum([portions[i] for i in free]), rest
        for i in free:
            extra = min(limit - holding[i], max(1, left * portions[i] // mass), rest)
            holding[i] = holding[i] + extra
            rest = rest - extra
    return np.array(holding)


def gaussian(rng, dims, deviation, reach, shards=(), kind=jnp.bfloat16):
    values = deviation * jax.random.normal(rng, dims, jnp.float32)
    if shards:
        values = values * shard_levels(rng, dims, shards, -0.22, 0.18)
    return jnp.clip(values, -reach, reach).astype(kind)


def setup_inputs(seed: int = 0) -> dict:
    key_of = jax.random.split(jax.random.key(seed), 6)
    recording = draw_recording(jax.random.fold_in(key_of[5], 71), 0)
    start_vectors = gaussian(key_of[1], (PLANES, PATCHES, RANK, FRAMES), 1.0, 5.0, ((0, 4), (1, 8)), jnp.float32)
    footprints = jnp.clip(jnp.exp(math.log(0.029907227) - 5.0109542 * jax.random.uniform(key_of[2], (PLANES, SRC, BLK), jnp.float32) ** shard_levels(key_of[2], (PLANES, SRC, BLK), ((0, 4), (1, 8)), -0.2, 0.2)), 0.00019931793, 0.029907227).astype(jnp.bfloat16)
    source_row_keys = jax.random.split(jax.random.fold_in(key_of[3], 1), PLANES * SRC // SRC_DEV)
    source_row_turns = jax.random.permutation(jax.random.fold_in(key_of[3], 3), PLANES * SRC // SRC_DEV)
    source_row = jax.vmap(lambda own, number: routed_block(jax.random.fold_in(key_of[3], 2), own, number, SRC_DEV, N_TILE - 2, 1, MOST, 2))(source_row_keys, source_row_turns).reshape((PLANES, SRC, 1))
    footprint_block = touch_ends(jax.random.randint(key_of[4], (PLANES, SRC), 0, 4 * (P_DEV - 1)), jax.random.fold_in(key_of[4], 1), 0, (4 * (P_DEV - 1)) - 1).astype(jnp.int32)
    return dict(recording=recording, start_vectors=start_vectors, footprints=footprints, source_row=source_row, footprint_block=footprint_block)


def compress_patches(patches, start_block):
    temporal = start_block
    spatial = None
    for step_index in range(ITERS):
        temporal_bf = lax.optimization_barrier(temporal.astype(jnp.bfloat16)).astype(jnp.float32)
        projection = jnp.einsum('prf,pkf->prk', temporal_bf, patches, precision=lax.Precision.HIGHEST)
        gram_matrix = jnp.einsum('prk,psk->prs', projection, projection, precision=lax.Precision.HIGHEST)
        cholesky_factor = jnp.linalg.cholesky(gram_matrix)
        spatial = jax.scipy.linalg.solve_triangular(cholesky_factor, projection, lower=True).astype(jnp.bfloat16)
        spatial = lax.optimization_barrier(spatial)
        temporal = jnp.einsum('prk,pkf->prf', spatial.astype(jnp.float32), patches, precision=lax.Precision.HIGHEST)
    return (spatial, temporal)

def reference(recording, start_vectors, footprints, source_row, footprint_block):
    pixel_total = PLANES * TILES * CELLS * 4 * BLK
    frame_sums = jnp.sum(recording, axis=(0, 1, 2, 3, 4), dtype=jnp.float32)
    background = frame_sums / pixel_total
    strip_valid = jnp.arange(TILES) < TILES - 2

    def one_strip(inputs):
        own_strip, next_strip, valid_flag, start_block = inputs
        centered = (own_strip.astype(jnp.float32) - background).astype(jnp.bfloat16)
        centered = lax.optimization_barrier(centered)
        lower_strip = jnp.where(valid_flag, next_strip.astype(jnp.float32) - background, 0.0).astype(jnp.bfloat16)
        lower_strip = lax.optimization_barrier(lower_strip)
        stacked = jnp.stack([centered, lower_strip])
        patches = jnp.stack([stacked[:, column_index:column_index + 2].reshape(16 * BLK, FRAMES) for column_index in range(P_DEV)]).astype(jnp.float32)
        return compress_patches(patches, start_block)

    def one_plane(inputs):
        plane_data, plane_start = inputs
        shifted = jnp.concatenate([plane_data[2:], jnp.zeros_like(plane_data[:2])], 0)
        return lax.map(one_strip, (plane_data, shifted, strip_valid, plane_start.reshape(TILES, P_DEV, RANK, FRAMES)))
    spatial_all, temporal_all = lax.map(one_plane, (recording, start_vectors))
    temporal_factors = temporal_all.reshape(PLANES, PATCHES, RANK, FRAMES)
    spatial_blocks = spatial_all.reshape(PLANES, PATCHES, RANK, 16, BLK)
    temporal_rounded = lax.optimization_barrier(temporal_factors.astype(jnp.bfloat16))

    def plane_traces(inputs):
        blocks_here, rounded_here, weights_here, rows_here, codes_here = inputs
        row_value = rows_here[:, 0].astype(jnp.int32)
        column_cell = codes_here // 4 + 1
        quarter = codes_here % 4
        patch_ids = jnp.stack([row_value * P_DEV + column_cell - 1, row_value * P_DEV + column_cell, (row_value + 2) * P_DEV + column_cell - 1, (row_value + 2) * P_DEV + column_cell], 1).astype(jnp.int32)
        block_ids = jnp.stack([12 + quarter, 8 + quarter, 4 + quarter, quarter], 1).astype(jnp.int32)

        def source_group(group):
            weight_rows, patch_group, block_group = group
            columns = blocks_here[patch_group, :, block_group].astype(jnp.float32)
            coefficient = jnp.einsum('sk,sjrk->sjr', weight_rows.astype(jnp.float32), columns, precision=lax.Precision.HIGHEST)
            coefficient = lax.optimization_barrier(coefficient.astype(jnp.bfloat16)).astype(jnp.float32)
            temporal_rows = rounded_here[patch_group].astype(jnp.float32)
            return 0.25 * jnp.einsum('sjr,sjrf->sf', coefficient, temporal_rows, precision=lax.Precision.HIGHEST)
        grouped = lax.map(source_group, (weights_here.reshape(N_TILE, SRC_DEV, BLK), patch_ids.reshape(N_TILE, SRC_DEV, 4), block_ids.reshape(N_TILE, SRC_DEV, 4)))
        return grouped.reshape(SRC, FRAMES)
    traces = lax.map(plane_traces, (spatial_blocks, temporal_rounded, footprints, source_row, footprint_block))
    return (temporal_factors, traces)
```

```python
import jax
import jax.numpy as jnp
from jax import lax
from jax.experimental import pallas as pl
from jax.experimental.pallas import tpu as pltpu
from jax.sharding import PartitionSpec as P

ITERS = 3
CODE_ROWS = 16
EXACT = lax.Precision.HIGHEST


def from_behind(block, axis, distance):
    devices = range(lax.axis_size(axis))
    route = [(i - distance, i) for i in devices if i - distance in devices]
    return lax.ppermute(block, axis, route)


def vmem_call(body, outs, name, flops, nbytes, in_specs=None, limit=None):
    params = pltpu.CompilerParams() if limit is None else pltpu.CompilerParams(vmem_limit_bytes=limit)
    extra = {} if in_specs is None else {"in_specs": in_specs}
    return pl.pallas_call(
        body,
        out_shape=outs,
        name=name,
        compiler_params=params,
        cost_estimate=pl.CostEstimate(flops=flops, bytes_accessed=nbytes, transcendentals=0),
        **extra,
    )


def rows_dot(left, right, precision=None):
    return lax.dot_general(
        left, right, (((1,), (1,)), ((), ())), precision=precision, preferred_element_type=jnp.float32
    )


def columns_dot(left, right):
    return lax.dot_general(left, right, (((0,), (0,)), ((), ())), preferred_element_type=jnp.float32)


def sum_body(strip_ref, row_ref, block_ref, footprint_ref, sums_ref, middle_ref, shared_ref):
    rows = strip_ref.shape[0]
    ones = jnp.ones((8, rows), jnp.bfloat16)
    total = jnp.dot(ones, strip_ref[...], preferred_element_type=jnp.float32)
    sums_ref[...] = jnp.broadcast_to(total[0:1], sums_ref.shape)
    cell = middle_ref.shape[0]
    middle_ref[...] = strip_ref[cell : 2 * cell, :]
    sources = footprint_ref.shape[0]
    shared_ref[0:sources, :] = footprint_ref[...]
    codes = jnp.concatenate([row_ref[...], block_ref[...]], 1).astype(jnp.float32)
    shared_ref[sources:, :] = jnp.broadcast_to(codes, (CODE_ROWS, codes.shape[1])).astype(jnp.bfloat16)


def gram_body(pixel_total, sums_ref, strip_ref, gram_ref, middle_ref):
    background = jnp.sum(sums_ref[...], axis=0, keepdims=True) / pixel_total
    cell = middle_ref.shape[0]
    cells = strip_ref.shape[0] // cell
    grams = []
    for index in range(cells):
        raw = strip_ref[index * cell : (index + 1) * cell, :].astype(jnp.float32)
        centered = (raw - background).astype(jnp.bfloat16)
        if index == 1:
            middle_ref[...] = centered
        grams.append(columns_dot(centered, centered))
    for column in range(cells - 1):
        gram_ref[column] = grams[column] + grams[column + 1]


def forward_solve(grams, sides):
    rank = grams[0].shape[0]
    blocks = rank // 8
    width = 128
    sub = lax.broadcasted_iota(jnp.int32, (8, width), 0)
    pad = jnp.zeros((rank, width - rank), jnp.float32)
    grams = [jnp.concatenate([gram, pad], 1) for gram in grams]

    def split(matrix):
        return [matrix[8 * b : 8 * b + 8] for b in range(blocks)]

    grams = [split(gram) for gram in grams]
    sides = [[split(side) for side in group] for group in sides]
    inverse = [[None] * blocks for _ in grams]
    for block in range(blocks):
        columns = [
            {
                (j, b): jnp.broadcast_to(gram[b][:, 8 * block + j : 8 * block + j + 1], (8, width))
                for j in range(8)
                for b in range(block, blocks)
            }
            for gram in grams
        ]
        for j in range(8):
            for patch in range(len(grams)):
                column, gram = columns[patch], grams[patch]
                pivot = 1.0 / jnp.broadcast_to(column[(j, block)][j : j + 1, :], (8, width))
                known = inverse[patch][block]
                inverse[patch][block] = pivot if known is None else jnp.where(sub == j, pivot, known)
                factor = {b: column[(j, b)] * pivot for b in range(block, blocks)}
                factor[block] = jnp.where(sub > j, factor[block], 0.0)
                for later in range(j + 1, 8):
                    entry = jnp.broadcast_to(column[(j, block)][later : later + 1, :], (8, width))
                    for b in range(block, blocks):
                        column[(later, b)] = column[(later, b)] - factor[b] * entry
                for target in [gram] + sides[patch]:
                    row = jnp.broadcast_to(target[block][j : j + 1, :], (8, width))
                    for b in range(block, blocks):
                        target[b] = target[b] - factor[b] * row
    return [
        [
            jnp.concatenate([m * lax.sqrt(d) for m, d in zip(side, inverse[patch])], 0)
            for side in group
        ]
        for patch, group in enumerate(sides)
    ]


def three_parts(value):
    high = value.astype(jnp.bfloat16)
    rest = value - high.astype(jnp.float32)
    middle = rest.astype(jnp.bfloat16)
    low = (rest - middle.astype(jnp.float32)).astype(jnp.bfloat16)
    return [high, middle, low]


def patch_body(
    pixel_total, place_ref, own_gram_ref, low_gram_ref, sums_ref, own_ref, low_ref, start_ref,
    shared_ref, temporal_ref, reply_ref,
):
    patches, rank = start_ref.shape[0], start_ref.shape[1]
    grams = [own_gram_ref[p] + low_gram_ref[p] for p in range(patches)]
    temporal = [start_ref[p] for p in range(patches)]
    whitened = None
    for step in range(ITERS):
        rounded = [t.astype(jnp.bfloat16).astype(jnp.float32) for t in temporal]
        moved = [jnp.dot(t, g, precision=EXACT, preferred_element_type=jnp.float32) for t, g in zip(rounded, grams)]
        inner = [rows_dot(m, t, EXACT) for m, t in zip(moved, rounded)]
        last = step == ITERS - 1
        solved = forward_solve(inner, [[m, t] if last else [m] for m, t in zip(moved, rounded)])
        temporal = [s[0] for s in solved]
        if last:
            whitened = jnp.concatenate([s[1] for s in solved], 0)
    for p in range(patches):
        temporal_ref[p] = temporal[p]
    ranks = patches * rank
    temporal_rounded = jnp.concatenate(temporal, 0).astype(jnp.bfloat16)
    background = jnp.sum(sums_ref[...], axis=0, keepdims=True) / pixel_total
    lower = (low_ref[...].astype(jnp.float32) - background).astype(jnp.bfloat16)
    parts = jnp.concatenate(three_parts(whitened), 0)
    pixels = 256
    bands = []
    for centered in (lower, own_ref[...]):
        sums = rows_dot(parts, centered)
        spatial = (sums[:ranks] + sums[ranks : 2 * ranks] + sums[2 * ranks :]).astype(jnp.bfloat16)
        bands += [spatial[:, q * pixels : (q + 1) * pixels] for q in range(4)]
    stacked = jnp.concatenate(bands, 0)
    place = place_ref[0]
    owners, sources = reply_ref.shape[0], reply_ref.shape[2]

    def one_owner(owner):
        projected = rows_dot(stacked, shared_ref[owner, 0:sources, :])
        codes = shared_ref[owner, sources : sources + 1, :].astype(jnp.float32)
        code_row = codes[:, 0:sources].astype(jnp.int32)
        code_quarter = codes[:, sources : 2 * sources].astype(jnp.int32)
        total = jnp.zeros((ranks, sources), jnp.float32)
        for role in range(2):
            for quarter in range(4):
                start = (role * 4 + quarter) * ranks
                chosen = (code_row == place - 2 * role) & (code_quarter == quarter)
                total = total + jnp.where(chosen, projected[start : start + ranks], 0.0)
        reply_ref[owner, 0:ranks, :] = total.astype(jnp.bfloat16)
        reply_ref[owner, ranks:, :] = temporal_rounded

    if owners <= 8:
        for owner in range(owners):
            one_owner(owner)
    else:
        pl.loop(0, owners)(one_owner)


def trace_body(reply_ref, traces_ref):
    owners, rows = reply_ref.shape[0], reply_ref.shape[1]
    ranks = rows // 2
    group = min(owners, 8)

    def one_group(first):
        coefficient = reply_ref[pl.ds(first, group), 0:ranks, :].reshape(group * ranks, -1)
        temporal = reply_ref[pl.ds(first, group), ranks:, :].reshape(group * ranks, -1)
        return columns_dot(coefficient, temporal)

    if owners == group:
        traces_ref[...] = 0.25 * one_group(0)
    else:
        traces_ref[...] = lax.fori_loop(
            0, owners // group, lambda i, total: total + 0.25 * one_group(i * group), jnp.zeros_like(traces_ref[...])
        )


def on_device(recording, start_vectors, footprints, source_row, footprint_block):
    tile_count = lax.axis_size("tile")
    plane_count = lax.axis_size("plane")
    devices = tile_count * plane_count
    cells, quarters, pixels, frames = recording.shape[2:]
    cell = quarters * pixels
    strip = recording.reshape(cells * cell, frames)
    start = start_vectors[0]
    patches, rank = start.shape[0], start.shape[1]
    sources = footprints.shape[1]
    pixel_total = devices * cells * cell
    f32, bf16 = jnp.float32, jnp.bfloat16

    def shape(dims, kind):
        return jax.ShapeDtypeStruct(dims, kind)

    sums, middle, shared = vmem_call(
        sum_body,
        [shape((devices, frames), f32), shape((cell, frames), bf16), shape((sources + CODE_ROWS, pixels), bf16)],
        "frame_sums",
        2 * cells * cell * frames,
        2 * cells * cell * frames,
    )(strip, source_row.reshape(1, sources), footprint_block.reshape(1, sources), footprints[0])
    all_sums = lax.all_to_all(sums, ("plane", "tile"), 0, 0, tiled=True)
    shared_all = lax.all_gather(shared, "tile", axis=0)
    low_middle = from_behind(middle, "tile", -2)
    own_gram, own_middle = vmem_call(
        lambda *refs: gram_body(pixel_total, *refs),
        [shape((patches, frames, frames), f32), shape((cell, frames), bf16)],
        "own_grams",
        2 * cells * cell * frames * frames,
        2 * cells * cell * frames,
    )(all_sums, strip)
    low_gram = from_behind(own_gram, "tile", -2)
    place = lax.axis_index("tile").astype(jnp.int32).reshape(1)
    whole = pl.BlockSpec(memory_space=pltpu.VMEM)
    temporal, reply = vmem_call(
        lambda *refs: patch_body(pixel_total, *refs),
        [shape((patches, rank, frames), f32), shape((tile_count, 2 * patches * rank, sources), bf16)],
        "patch_factors",
        2 * 1024 * 512 * 256,
        4 << 20,
        in_specs=[pl.BlockSpec(memory_space=pltpu.SMEM)] + [whole] * 7,
        limit=None if tile_count <= 8 else 40 << 20,
    )(place, own_gram, low_gram, all_sums, own_middle, low_middle, start, shared_all)
    answers = lax.all_to_all(reply, "tile", 0, 0, tiled=True)
    traces = vmem_call(
        trace_body,
        shape((sources, frames), f32),
        "source_traces",
        2 * sources * frames * patches * rank * tile_count,
        2 * answers.size,
    )(answers)
    return (temporal[None], traces[None])


def solution(mesh):
    placed = (
        P("plane", "tile", None, None, None, None),
        P("plane", "tile", None, None),
        P("plane", "tile", None),
        P("plane", "tile", None),
        P("plane", "tile"),
    )
    return jax.shard_map(
        on_device,
        mesh=mesh,
        in_specs=placed,
        out_specs=(P("plane", "tile", None, None), P("plane", "tile", None)),
        check_vma=False,
    )
```

```python
import jax
import jax.numpy as jnp
from jax import lax
from jax.experimental import pallas as pl
from jax.experimental.pallas import tpu as pltpu
from jax.sharding import PartitionSpec as P

ITERS = 3
CODE_ROWS = 16
EXACT = lax.Precision.HIGHEST


def from_behind(block, axis, distance):
    devices = range(lax.axis_size(axis))
    route = [(i - distance, i) for i in devices if i - distance in devices]
    return lax.ppermute(block, axis, route)


def vmem_call(body, outs, name, flops, nbytes, in_specs=None, limit=None):
    params = pltpu.CompilerParams(vmem_limit_bytes=12 << 20) if limit is None else pltpu.CompilerParams(vmem_limit_bytes=limit)
    extra = {} if in_specs is None else {"in_specs": in_specs}
    return pl.pallas_call(
        body,
        out_shape=outs,
        name=name,
        compiler_params=params,
        cost_estimate=pl.CostEstimate(flops=flops, bytes_accessed=nbytes, transcendentals=0),
        **extra,
    )


def rows_dot(left, right, precision=None):
    return lax.dot_general(
        left, right, (((1,), (1,)), ((), ())), precision=precision, preferred_element_type=jnp.float32
    )


def columns_dot(left, right):
    return lax.dot_general(left, right, (((0,), (0,)), ((), ())), preferred_element_type=jnp.float32)


def sum_body(strip_ref, row_ref, block_ref, footprint_ref, sums_ref, middle_ref, shared_ref):
    rows = strip_ref.shape[0]
    ones = jnp.ones((8, rows), jnp.bfloat16)
    total = jnp.dot(ones, strip_ref[...], preferred_element_type=jnp.float32)
    sums_ref[...] = jnp.broadcast_to(total[0:1], sums_ref.shape)
    cell = middle_ref.shape[0]
    middle_ref[...] = strip_ref[cell : 2 * cell, :]
    sources = footprint_ref.shape[0]
    shared_ref[0:sources, :] = footprint_ref[...]
    codes = jnp.concatenate([row_ref[...], block_ref[...]], 1).astype(jnp.float32)
    shared_ref[sources:, :] = jnp.broadcast_to(codes, (CODE_ROWS, codes.shape[1])).astype(jnp.bfloat16)


def gram_body(pixel_total, sums_ref, strip_ref, gram_ref, middle_ref):
    background = jnp.sum(sums_ref[...], axis=0, keepdims=True) / pixel_total
    cell = middle_ref.shape[0]
    cells = strip_ref.shape[0] // cell
    grams = []
    for index in range(cells):
        raw = strip_ref[index * cell : (index + 1) * cell, :].astype(jnp.float32)
        centered = (raw - background).astype(jnp.bfloat16)
        if index == 1:
            middle_ref[...] = centered
        grams.append(columns_dot(centered, centered))
    for column in range(cells - 1):
        gram_ref[column] = grams[column] + grams[column + 1]


def forward_solve(grams, sides):
    rank = grams[0].shape[0]
    blocks = rank // 8
    width = 128
    sub = lax.broadcasted_iota(jnp.int32, (8, width), 0)
    pad = jnp.zeros((rank, width - rank), jnp.float32)
    grams = [jnp.concatenate([gram, pad], 1) for gram in grams]

    def split(matrix):
        return [matrix[8 * b : 8 * b + 8] for b in range(blocks)]

    grams = [split(gram) for gram in grams]
    sides = [[split(side) for side in group] for group in sides]
    inverse = [[None] * blocks for _ in grams]
    for block in range(blocks):
        columns = [
            {
                (j, b): jnp.broadcast_to(gram[b][:, 8 * block + j : 8 * block + j + 1], (8, width))
                for j in range(8)
                for b in range(block, blocks)
            }
            for gram in grams
        ]
        for j in range(8):
            for patch in range(len(grams)):
                column, gram = columns[patch], grams[patch]
                pivot = 1.0 / jnp.broadcast_to(column[(j, block)][j : j + 1, :], (8, width))
                known = inverse[patch][block]
                inverse[patch][block] = pivot if known is None else jnp.where(sub == j, pivot, known)
                factor = {b: column[(j, b)] * pivot for b in range(block, blocks)}
                factor[block] = jnp.where(sub > j, factor[block], 0.0)
                for later in range(j + 1, 8):
                    entry = jnp.broadcast_to(column[(j, block)][later : later + 1, :], (8, width))
                    for b in range(block, blocks):
                        column[(later, b)] = column[(later, b)] - factor[b] * entry
                for target in [gram] + sides[patch]:
                    row = jnp.broadcast_to(target[block][j : j + 1, :], (8, width))
                    for b in range(block, blocks):
                        target[b] = target[b] - factor[b] * row
    return [
        [
            jnp.concatenate([m * lax.sqrt(d) for m, d in zip(side, inverse[patch])], 0)
            for side in group
        ]
        for patch, group in enumerate(sides)
    ]


def three_parts(value):
    high = value.astype(jnp.bfloat16)
    rest = value - high.astype(jnp.float32)
    middle = rest.astype(jnp.bfloat16)
    low = (rest - middle.astype(jnp.float32)).astype(jnp.bfloat16)
    return [high, middle, low]


def patch_body(own_gram_ref, low_gram_ref, start_ref, temporal_ref, parts_ref, rounded_ref):
    patches = start_ref.shape[0]
    grams = [own_gram_ref[p] + low_gram_ref[p] for p in range(patches)]
    temporal = [start_ref[p] for p in range(patches)]
    whitened = None
    for step in range(ITERS):
        rounded = [t.astype(jnp.bfloat16).astype(jnp.float32) for t in temporal]
        moved = [jnp.dot(t, g, precision=EXACT, preferred_element_type=jnp.float32) for t, g in zip(rounded, grams)]
        inner = [rows_dot(m, t, EXACT) for m, t in zip(moved, rounded)]
        last = step == ITERS - 1
        solved = forward_solve(inner, [[m, t] if last else [m] for m, t in zip(moved, rounded)])
        temporal = [s[0] for s in solved]
        if last:
            whitened = jnp.concatenate([s[1] for s in solved], 0)
    for p in range(patches):
        temporal_ref[p] = temporal[p]
    rounded_ref[...] = jnp.concatenate(temporal, 0).astype(jnp.bfloat16)
    parts_ref[...] = jnp.concatenate(three_parts(whitened), 0)


def reply_body(pixel_total, place_ref, parts_ref, rounded_ref, sums_ref, own_ref, low_ref, *refs):
    shared_refs, reply_ref = refs[:-1], refs[-1]
    parts = parts_ref[...]
    temporal_rounded = rounded_ref[...]
    ranks = temporal_rounded.shape[0]
    background = jnp.sum(sums_ref[...], axis=0, keepdims=True) / pixel_total
    lower = (low_ref[...].astype(jnp.float32) - background).astype(jnp.bfloat16)
    pixels = 256
    bands = []
    for centered in (lower, own_ref[...]):
        sums = rows_dot(parts, centered)
        spatial = (sums[:ranks] + sums[ranks : 2 * ranks] + sums[2 * ranks :]).astype(jnp.bfloat16)
        bands += [spatial[:, q * pixels : (q + 1) * pixels] for q in range(4)]
    stacked = jnp.concatenate(bands, 0)
    place = place_ref[0]
    owners, sources = reply_ref.shape[0], reply_ref.shape[2]

    bits = owners.bit_length() - 1

    def one_owner(shared_ref, entry, order):
        offset = sum(((order >> t) & 1) << (bits - 1 - t) for t in range(bits))
        owner = lax.bitwise_xor(place, jnp.int32(offset))
        projected = rows_dot(stacked, shared_ref[entry, 0:sources, :])
        codes = shared_ref[entry, sources : sources + 1, :].astype(jnp.float32)
        code_row = codes[:, 0:sources].astype(jnp.int32)
        code_quarter = codes[:, sources : 2 * sources].astype(jnp.int32)
        total = jnp.zeros((ranks, sources), jnp.float32)
        for role in range(2):
            for quarter in range(4):
                start = (role * 4 + quarter) * ranks
                chosen = (code_row == place - 2 * role) & (code_quarter == quarter)
                total = total + jnp.where(chosen, projected[start : start + ranks], 0.0)
        reply_ref[owner, 0:ranks, :] = total.astype(jnp.bfloat16)
        reply_ref[owner, ranks:, :] = temporal_rounded

    offset = 0
    for shared_ref in shared_refs:
        count = shared_ref.shape[0]
        if owners <= 8:
            for entry in range(count):
                one_owner(shared_ref, entry, offset + entry)
        else:
            pl.loop(0, count)(lambda entry, ref=shared_ref, first=offset: one_owner(ref, entry, first + entry))
        offset += count


def trace_body(reply_ref, traces_ref):
    owners, rows = reply_ref.shape[0], reply_ref.shape[1]
    ranks = rows // 2
    group = min(owners, 8)

    def one_group(first):
        coefficient = reply_ref[pl.ds(first, group), 0:ranks, :].reshape(group * ranks, -1)
        temporal = reply_ref[pl.ds(first, group), ranks:, :].reshape(group * ranks, -1)
        return columns_dot(coefficient, temporal)

    if owners == group:
        traces_ref[...] = 0.25 * one_group(0)
    else:
        traces_ref[...] = lax.fori_loop(
            0, owners // group, lambda i, total: total + 0.25 * one_group(i * group), jnp.zeros_like(traces_ref[...])
        )


def on_device(recording, start_vectors, footprints, source_row, footprint_block):
    tile_count = lax.axis_size("tile")
    plane_count = lax.axis_size("plane")
    devices = tile_count * plane_count
    cells, quarters, pixels, frames = recording.shape[2:]
    cell = quarters * pixels
    strip = recording.reshape(cells * cell, frames)
    start = start_vectors[0]
    patches, rank = start.shape[0], start.shape[1]
    sources = footprints.shape[1]
    pixel_total = devices * cells * cell
    f32, bf16 = jnp.float32, jnp.bfloat16

    def shape(dims, kind):
        return jax.ShapeDtypeStruct(dims, kind)

    sums, middle, shared = vmem_call(
        sum_body,
        [shape((devices, frames), f32), shape((cell, frames), bf16), shape((sources + CODE_ROWS, pixels), bf16)],
        "frame_sums",
        2 * cells * cell * frames,
        2 * cells * cell * frames,
    )(strip, source_row.reshape(1, sources), footprint_block.reshape(1, sources), footprints[0])
    all_sums = lax.all_to_all(sums, ("plane", "tile"), 0, 0, tiled=True)
    low_middle = from_behind(middle, "tile", -2)
    own_gram, own_middle = vmem_call(
        lambda *refs: gram_body(pixel_total, *refs),
        [shape((patches, frames, frames), f32), shape((cell, frames), bf16)],
        "own_grams",
        2 * cells * cell * frames * frames,
        2 * cells * cell * frames,
    )(all_sums, strip)
    low_gram = from_behind(own_gram, "tile", -2)
    held = [shared[None]]
    bits = tile_count.bit_length() - 1
    for bit in reversed(range(bits)):
        route = [(i, i ^ (1 << bit)) for i in range(tile_count)]
        everything = held[0] if len(held) == 1 else jnp.concatenate(held, 0)
        if len(held) == 2:
            everything, own_gram = lax.optimization_barrier((everything, own_gram))
        held.append(lax.ppermute(everything, "tile", route))
    place = lax.axis_index("tile").astype(jnp.int32).reshape(1)
    whole = pl.BlockSpec(memory_space=pltpu.VMEM)
    ranks = patches * rank
    temporal, parts, rounded = vmem_call(
        patch_body,
        [shape((patches, rank, frames), f32), shape((3 * ranks, frames), bf16), shape((ranks, frames), bf16)],
        "patch_factors",
        6 * 10**9,
        1 << 20,
    )(own_gram, low_gram, start)
    (reply,) = vmem_call(
        lambda *refs: reply_body(pixel_total, *refs),
        [shape((tile_count, 2 * ranks, sources), bf16)],
        "coefficients",
        2 * 1024 * 512 * 256,
        2 << 20,
        in_specs=[pl.BlockSpec(memory_space=pltpu.SMEM)] + [whole] * (5 + len(held)),
        limit=None if tile_count <= 8 else 40 << 20,
    )(place, parts, rounded, all_sums, own_middle, low_middle, *held)
    answers = lax.all_to_all(reply, "tile", 0, 0, tiled=True)
    traces = vmem_call(
        trace_body,
        shape((sources, frames), f32),
        "source_traces",
        2 * sources * frames * patches * rank * tile_count,
        2 * answers.size,
    )(answers)
    return (temporal[None], traces[None])


def solution(mesh):
    placed = (
        P("plane", "tile", None, None, None, None),
        P("plane", "tile", None, None),
        P("plane", "tile", None),
        P("plane", "tile", None),
        P("plane", "tile"),
    )
    return jax.shard_map(
        on_device,
        mesh=mesh,
        in_specs=placed,
        out_specs=(P("plane", "tile", None, None), P("plane", "tile", None)),
        check_vma=False,
    )
```

```python
import jax
import jax.numpy as jnp
from jax import lax
from jax.experimental import pallas as pl
from jax.experimental.pallas import tpu as pltpu
from jax.sharding import PartitionSpec as P

ITERS = 3
EXACT = lax.Precision.HIGHEST


def from_behind(block, axis, distance):
    devices = range(lax.axis_size(axis))
    route = [(i - distance, i) for i in devices if i - distance in devices]
    return lax.ppermute(block, axis, route)


def vmem_call(body, outs, name, flops, nbytes, in_specs=None, limit=None):
    params = pltpu.CompilerParams(vmem_limit_bytes=12 << 20) if limit is None else pltpu.CompilerParams(vmem_limit_bytes=limit)
    extra = {} if in_specs is None else {"in_specs": in_specs}
    return pl.pallas_call(
        body,
        out_shape=outs,
        name=name,
        compiler_params=params,
        cost_estimate=pl.CostEstimate(flops=flops, bytes_accessed=nbytes, transcendentals=0),
        **extra,
    )


def rows_dot(left, right, precision=None):
    return lax.dot_general(
        left, right, (((1,), (1,)), ((), ())), precision=precision, preferred_element_type=jnp.float32
    )


def columns_dot(left, right):
    return lax.dot_general(left, right, (((0,), (0,)), ((), ())), preferred_element_type=jnp.float32)


def sum_body(strip_ref, sums_ref, middle_ref):
    rows = strip_ref.shape[0]
    ones = jnp.ones((8, rows), jnp.bfloat16)
    sums_ref[...] = jnp.dot(ones, strip_ref[...], preferred_element_type=jnp.float32)
    cell = middle_ref.shape[0]
    middle_ref[...] = strip_ref[cell : 2 * cell, :]


def background_of(notes_ref, frames, pixel_total):
    return jnp.sum(notes_ref[:, 0:frames], axis=0, keepdims=True) / pixel_total


def gram_body(pixel_total, notes_ref, strip_ref, gram_ref, middle_ref):
    background = background_of(notes_ref, strip_ref.shape[1], pixel_total)
    cell = middle_ref.shape[0]
    cells = strip_ref.shape[0] // cell
    grams = []
    for index in range(cells):
        raw = strip_ref[index * cell : (index + 1) * cell, :].astype(jnp.float32)
        centered = (raw - background).astype(jnp.bfloat16)
        if index == 1:
            middle_ref[...] = centered
        grams.append(columns_dot(centered, centered))
    for column in range(cells - 1):
        gram_ref[column] = grams[column] + grams[column + 1]


def forward_solve(grams, sides):
    rank = grams[0].shape[0]
    blocks = rank // 8
    width = 128
    sub = lax.broadcasted_iota(jnp.int32, (8, width), 0)
    pad = jnp.zeros((rank, width - rank), jnp.float32)
    grams = [jnp.concatenate([gram, pad], 1) for gram in grams]

    def split(matrix):
        return [matrix[8 * b : 8 * b + 8] for b in range(blocks)]

    grams = [split(gram) for gram in grams]
    sides = [[split(side) for side in group] for group in sides]
    inverse = [[None] * blocks for _ in grams]
    for block in range(blocks):
        columns = [
            {
                (j, b): jnp.broadcast_to(gram[b][:, 8 * block + j : 8 * block + j + 1], (8, width))
                for j in range(8)
                for b in range(block, blocks)
            }
            for gram in grams
        ]
        for j in range(8):
            for patch in range(len(grams)):
                column, gram = columns[patch], grams[patch]
                pivot = 1.0 / jnp.broadcast_to(column[(j, block)][j : j + 1, :], (8, width))
                known = inverse[patch][block]
                inverse[patch][block] = pivot if known is None else jnp.where(sub == j, pivot, known)
                factor = {b: column[(j, b)] * pivot for b in range(block, blocks)}
                factor[block] = jnp.where(sub > j, factor[block], 0.0)
                for later in range(j + 1, 8):
                    entry = jnp.broadcast_to(column[(j, block)][later : later + 1, :], (8, width))
                    for b in range(block, blocks):
                        column[(later, b)] = column[(later, b)] - factor[b] * entry
                for target in [gram] + sides[patch]:
                    row = jnp.broadcast_to(target[block][j : j + 1, :], (8, width))
                    for b in range(block, blocks):
                        target[b] = target[b] - factor[b] * row
    return [
        [
            jnp.concatenate([m * lax.sqrt(d) for m, d in zip(side, inverse[patch])], 0)
            for side in group
        ]
        for patch, group in enumerate(sides)
    ]


def three_parts(value):
    high = value.astype(jnp.bfloat16)
    rest = value - high.astype(jnp.float32)
    middle = rest.astype(jnp.bfloat16)
    low = (rest - middle.astype(jnp.float32)).astype(jnp.bfloat16)
    return [high, middle, low]


def patch_body(own_gram_ref, low_gram_ref, start_ref, temporal_ref, parts_ref, rounded_ref):
    patches = start_ref.shape[0]
    grams = [own_gram_ref[p] + low_gram_ref[p] for p in range(patches)]
    temporal = [start_ref[p] for p in range(patches)]
    whitened = None
    for step in range(ITERS):
        rounded = [t.astype(jnp.bfloat16).astype(jnp.float32) for t in temporal]
        moved = [jnp.dot(t, g, precision=EXACT, preferred_element_type=jnp.float32) for t, g in zip(rounded, grams)]
        inner = [rows_dot(m, t, EXACT) for m, t in zip(moved, rounded)]
        last = step == ITERS - 1
        solved = forward_solve(inner, [[m, t] if last else [m] for m, t in zip(moved, rounded)])
        temporal = [s[0] for s in solved]
        if last:
            whitened = jnp.concatenate([s[1] for s in solved], 0)
    for p in range(patches):
        temporal_ref[p] = temporal[p]
    rounded_ref[...] = jnp.concatenate(temporal, 0).astype(jnp.bfloat16)
    parts_ref[...] = jnp.concatenate(three_parts(whitened), 0)


def reply_body(pixel_total, place_ref, parts_ref, rounded_ref, notes_ref, own_ref, low_ref, *refs):
    tile_count, paired = refs[0], refs[1]
    refs = refs[2:]
    held_count = tile_count.bit_length()
    held_refs, reply_refs = refs[:held_count], refs[held_count:]
    parts = parts_ref[...]
    temporal_rounded = rounded_ref[...]
    ranks, frames = temporal_rounded.shape
    background = background_of(notes_ref, frames, pixel_total)
    lower = (low_ref[...].astype(jnp.float32) - background).astype(jnp.bfloat16)
    pixels = 256
    bands = []
    for centered in (lower, own_ref[...]):
        sums = rows_dot(parts, centered)
        spatial = (sums[:ranks] + sums[ranks : 2 * ranks] + sums[2 * ranks :]).astype(jnp.bfloat16)
        bands += [spatial[:, q * pixels : (q + 1) * pixels] for q in range(4)]
    stacked = jnp.concatenate(bands, 0)
    place = place_ref[0]
    plane_start = place_ref[1] * tile_count
    sources = held_refs[0].shape[1]
    bits = tile_count.bit_length() - 1

    def turned(order):
        return sum(((order >> t) & 1) << (bits - 1 - t) for t in range(bits))

    def coefficients(held_ref, entry, owner):
        projected = rows_dot(stacked, held_ref[entry])
        codes = notes_ref[pl.ds(plane_start + owner, 1), :][:, frames : frames + sources].astype(jnp.int32)
        total = jnp.zeros((ranks, sources), jnp.float32)
        for role in range(2):
            for quarter in range(4):
                start = (role * 4 + quarter) * ranks
                chosen = codes == 4 * (place - 2 * role) + quarter
                total = total + jnp.where(chosen, projected[start : start + ranks], 0.0)
        return total.astype(jnp.bfloat16)

    first = 0
    for held_ref in held_refs:
        count = held_ref.shape[0]
        if paired:
            for entry in range(count):
                offset = turned(first + entry)
                owner = lax.bitwise_xor(place, jnp.int32(offset))
                row = (offset % 2) * ranks
                reply_refs[offset // 2][row : row + ranks, :] = coefficients(held_ref, entry, owner)
        else:

            def one_owner(entry, held_ref=held_ref, first=first):
                owner = lax.bitwise_xor(place, turned(first + entry))
                reply_refs[0][owner, 0:ranks, :] = coefficients(held_ref, entry, owner)
                reply_refs[0][owner, ranks:, :] = temporal_rounded

            pl.loop(0, count)(one_owner)
        first += count
    if paired:
        for reply_ref in reply_refs:
            reply_ref[2 * ranks :, :] = temporal_rounded


def paired_trace_body(*refs):
    own_refs, mate_ref, traces_ref = refs[:-2], refs[-2], refs[-1]
    ranks = own_refs[0].shape[0] // 3
    coefficient = [r[0:ranks] for r in own_refs] + [mate_ref[i, 0:ranks] for i in range(len(own_refs))]
    temporal = [r[2 * ranks :] for r in own_refs] + [mate_ref[i, ranks:] for i in range(len(own_refs))]
    traces_ref[...] = 0.25 * columns_dot(jnp.concatenate(coefficient, 0), jnp.concatenate(temporal, 0))


def trace_body(reply_ref, traces_ref):
    owners, rows = reply_ref.shape[0], reply_ref.shape[1]
    ranks = rows // 2
    group = min(owners, 8)

    def one_group(first):
        coefficient = reply_ref[pl.ds(first, group), 0:ranks, :].reshape(group * ranks, -1)
        temporal = reply_ref[pl.ds(first, group), ranks:, :].reshape(group * ranks, -1)
        return columns_dot(coefficient, temporal)

    if owners == group:
        traces_ref[...] = 0.25 * one_group(0)
    else:
        traces_ref[...] = lax.fori_loop(
            0, owners // group, lambda i, total: total + 0.25 * one_group(i * group), jnp.zeros_like(traces_ref[...])
        )


def on_device(recording, start_vectors, footprints, source_row, footprint_block):
    tile_count = lax.axis_size("tile")
    plane_count = lax.axis_size("plane")
    devices = tile_count * plane_count
    cells, quarters, pixels, frames = recording.shape[2:]
    cell = quarters * pixels
    strip = recording.reshape(cells * cell, frames)
    start = start_vectors[0]
    patches, rank = start.shape[0], start.shape[1]
    sources = footprints.shape[1]
    pixel_total = devices * cells * cell
    f32, bf16 = jnp.float32, jnp.bfloat16

    def shape(dims, kind):
        return jax.ShapeDtypeStruct(dims, kind)

    sums, middle = vmem_call(
        sum_body,
        [shape((8, frames), f32), shape((cell, frames), bf16)],
        "frame_sums",
        2 * cells * cell * frames,
        2 * cells * cell * frames,
    )(strip)
    codes = (source_row.reshape(1, sources) * 4 + footprint_block.reshape(1, sources)).astype(f32)
    notes = jnp.broadcast_to(jnp.concatenate([sums[0:1], codes], 1), (devices, frames + sources))
    notes = lax.all_to_all(notes, ("plane", "tile"), 0, 0, tiled=True)
    low_middle = from_behind(middle, "tile", -2)
    own_gram, own_middle = vmem_call(
        lambda *refs: gram_body(pixel_total, *refs),
        [shape((patches, frames, frames), f32), shape((cell, frames), bf16)],
        "own_grams",
        2 * cells * cell * frames * frames,
        2 * cells * cell * frames,
    )(notes, strip)
    held = [footprints]
    for bit in reversed(range(tile_count.bit_length() - 1)):
        route = [(i, i ^ (1 << bit)) for i in range(tile_count)]
        everything = held[0] if len(held) == 1 else jnp.concatenate(held, 0)
        held.append(lax.ppermute(everything, "tile", route))
    low_gram = from_behind(own_gram, "tile", -2)
    place = jnp.stack([lax.axis_index("tile"), lax.axis_index("plane")]).astype(jnp.int32)
    whole = pl.BlockSpec(memory_space=pltpu.VMEM)
    ranks = patches * rank
    temporal, parts, rounded = vmem_call(
        patch_body,
        [shape((patches, rank, frames), f32), shape((3 * ranks, frames), bf16), shape((ranks, frames), bf16)],
        "patch_factors",
        6 * 10**9,
        1 << 20,
    )(own_gram, low_gram, start)
    chips = tile_count // 2
    paired = chips <= 4
    replies = vmem_call(
        lambda *refs: reply_body(pixel_total, *refs[:6], tile_count, paired, *refs[6:]),
        [shape((3 * ranks, sources), bf16)] * chips if paired else [shape((tile_count, 2 * ranks, sources), bf16)],
        "coefficients",
        2 * 1024 * 512 * 256,
        2 << 20,
        in_specs=[pl.BlockSpec(memory_space=pltpu.SMEM)] + [whole] * (5 + len(held)),
        limit=None if paired else 40 << 20,
    )(place, parts, rounded, notes, own_middle, low_middle, *held)
    flops = 2 * sources * frames * ranks * tile_count
    if paired:
        arrived = [replies[0]]
        for offset in range(1, chips):
            route = [(i, i ^ (2 * offset)) for i in range(tile_count)]
            arrived.append(lax.ppermute(replies[offset], "tile", route))
        handed = jnp.stack([block[ranks:] for block in arrived])
        mate = lax.ppermute(handed, "tile", [(i, i ^ 1) for i in range(tile_count)])
        traces = vmem_call(
            paired_trace_body, shape((sources, frames), f32), "source_traces", flops, 1 << 19
        )(*arrived, mate)
    else:
        answers = lax.all_to_all(replies[0], "tile", 0, 0, tiled=True)
        traces = vmem_call(trace_body, shape((sources, frames), f32), "source_traces", flops, 2 * answers.size)(answers)
    return (temporal[None], traces[None])


def solution(mesh):
    placed = (
        P("plane", "tile", None, None, None, None),
        P("plane", "tile", None, None),
        P("plane", "tile", None),
        P("plane", "tile", None),
        P("plane", "tile"),
    )
    return jax.shard_map(
        on_device,
        mesh=mesh,
        in_specs=placed,
        out_specs=(P("plane", "tile", None, None), P("plane", "tile", None)),
        check_vma=False,
    )
```

```python
import jax
import jax.numpy as jnp
from jax import lax
from jax.experimental import pallas as pl
from jax.experimental.pallas import tpu as pltpu
from jax.sharding import PartitionSpec as P

ITERS = 3


def from_behind(block, axis, distance):
    devices = range(lax.axis_size(axis))
    route = [(i - distance, i) for i in devices if i - distance in devices]
    return lax.ppermute(block, axis, route)


def vmem_call(body, outs, name, flops, nbytes, in_specs=None, limit=None, scratch=()):
    params = pltpu.CompilerParams(vmem_limit_bytes=12 << 20) if limit is None else pltpu.CompilerParams(vmem_limit_bytes=limit)
    extra = {} if in_specs is None else {"in_specs": in_specs}
    return pl.pallas_call(
        body,
        out_shape=outs,
        name=name,
        compiler_params=params,
        scratch_shapes=scratch,
        cost_estimate=pl.CostEstimate(flops=flops, bytes_accessed=nbytes, transcendentals=0),
        **extra,
    )


def rows_dot(left, right):
    return lax.dot_general(left, right, (((1,), (1,)), ((), ())), preferred_element_type=jnp.float32)


def columns_dot(left, right):
    return lax.dot_general(left, right, (((0,), (0,)), ((), ())), preferred_element_type=jnp.float32)


def sum_body(strip_ref, row_ref, block_ref, notes_ref, middle_ref, held_ref, codes_ref, strip_sems, code_sems):
    cell = middle_ref.shape[0]
    cells = strip_ref.shape[0] // cell
    copies = [
        pltpu.make_async_copy(
            strip_ref.at[pl.ds(i * cell, cell)], held_ref.at[pl.ds(i * cell, cell)], strip_sems.at[i]
        )
        for i in range(cells)
    ]
    code_copies = [
        pltpu.make_async_copy(source, codes_ref.at[pl.ds(i, 1)], code_sems.at[i])
        for i, source in enumerate((row_ref, block_ref))
    ]
    for copy in copies + code_copies:
        copy.start()
    ones = jnp.ones((8, cell), jnp.bfloat16)
    total = jnp.zeros((8, strip_ref.shape[1]), jnp.float32)
    for i in range(cells):
        copies[i].wait()
        piece = held_ref[i * cell : (i + 1) * cell, :]
        total = total + jnp.dot(ones, piece, preferred_element_type=jnp.float32)
        if i == 1:
            middle_ref[...] = piece
    for copy in code_copies:
        copy.wait()
    codes = (codes_ref[0:1, :] * 4 + codes_ref[1:2, :]).astype(jnp.float32)
    odd = lax.broadcasted_iota(jnp.int32, notes_ref.shape, 0) % 2 == 1
    notes_ref[...] = jnp.where(odd, codes, total[0:1])


def background_of(notes_ref, pixel_total):
    notes = notes_ref[...]
    even = lax.broadcasted_iota(jnp.int32, notes.shape, 0) % 2 == 0
    return jnp.sum(jnp.where(even, notes, 0.0), axis=0, keepdims=True) / pixel_total


def gram_body(pixel_total, notes_ref, strip_ref, gram_ref, middle_ref):
    background = background_of(notes_ref, pixel_total)
    cell = middle_ref.shape[0]
    cells = strip_ref.shape[0] // cell
    grams = []
    for index in range(cells):
        raw = strip_ref[index * cell : (index + 1) * cell, :].astype(jnp.float32)
        centered = (raw - background).astype(jnp.bfloat16)
        if index == 1:
            middle_ref[...] = centered
        grams.append(columns_dot(centered, centered))
    for column in range(cells - 1):
        gram_ref[column] = grams[column] + grams[column + 1]


def forward_solve(grams, sides, band=16):
    rank = grams[0].shape[0]
    blocks = rank // 8
    width = 128
    sub = lax.broadcasted_iota(jnp.int32, (8, width), 0)
    pad = jnp.zeros((rank, width - rank), jnp.float32)

    def split(matrix):
        return [matrix[8 * b : 8 * b + 8] for b in range(blocks)]

    def spread(row_or_column):
        return jnp.broadcast_to(row_or_column, (8, width))

    grams = [split(jnp.concatenate([gram, pad], 1)) for gram in grams]
    sides = [[split(side) for side in group] for group in sides]
    inverse = [[None] * blocks for _ in grams]
    for start in range(0, rank, band):
        columns = [
            {
                (j, b): spread(gram[b][:, start + j : start + j + 1])
                for j in range(band)
                for b in range((start + j) // 8, blocks)
            }
            for gram in grams
        ]
        for j in range(band):
            block, line = divmod(start + j, 8)
            for patch in range(len(grams)):
                column, gram = columns[patch], grams[patch]
                pivot = 1.0 / spread(column[(j, block)][line : line + 1, :])
                known = inverse[patch][block]
                inverse[patch][block] = pivot if known is None else jnp.where(sub == line, pivot, known)
                factor = {b: column[(j, b)] * pivot for b in range(block, blocks)}
                factor[block] = jnp.where(sub > line, factor[block], 0.0)
                for later in range(j + 1, band):
                    later_block, later_line = divmod(start + later, 8)
                    entry = spread(column[(j, later_block)][later_line : later_line + 1, :])
                    for b in range(later_block, blocks):
                        column[(later, b)] = column[(later, b)] - factor[b] * entry
                targets = sides[patch] if start + band == rank else [gram] + sides[patch]
                for target in targets:
                    row = spread(target[block][line : line + 1, :])
                    for b in range(block, blocks):
                        target[b] = target[b] - factor[b] * row
    return [
        [
            jnp.concatenate([m * lax.sqrt(d) for m, d in zip(side, inverse[patch])], 0)
            for side in group
        ]
        for patch, group in enumerate(sides)
    ]


def three_parts(value):
    high = value.astype(jnp.bfloat16)
    rest = value - high.astype(jnp.float32)
    middle = rest.astype(jnp.bfloat16)
    low = (rest - middle.astype(jnp.float32)).astype(jnp.bfloat16)
    return [high, middle, low]


def patch_body(own_gram_ref, low_gram_ref, start_ref, temporal_ref, parts_ref, rounded_ref):
    patches = start_ref.shape[0]
    grams = [
        jnp.concatenate(three_parts(own_gram_ref[p] + low_gram_ref[p]), 1) for p in range(patches)
    ]
    rank, frames = start_ref.shape[1], start_ref.shape[2]
    temporal = [start_ref[p] for p in range(patches)]
    whitened = None
    for step in range(ITERS):
        rounded = [t.astype(jnp.bfloat16) for t in temporal]
        moved, inner = [], []
        for narrow, gram in zip(rounded, grams):
            terms = jnp.dot(narrow, gram, preferred_element_type=jnp.float32)
            image = terms[:, :frames] + terms[:, frames : 2 * frames] + terms[:, 2 * frames :]
            terms = rows_dot(jnp.concatenate(three_parts(image), 0), narrow)
            moved.append(image)
            inner.append(terms[:rank] + terms[rank : 2 * rank] + terms[2 * rank :])
        last = step == ITERS - 1
        sides = [[m, t.astype(jnp.float32)] if last else [m] for m, t in zip(moved, rounded)]
        solved = forward_solve(inner, sides)
        temporal = [s[0] for s in solved]
        if last:
            whitened = jnp.concatenate([s[1] for s in solved], 0)
    for p in range(patches):
        temporal_ref[p] = temporal[p]
    rounded_ref[...] = jnp.concatenate(temporal, 0).astype(jnp.bfloat16)
    parts_ref[...] = jnp.concatenate(three_parts(whitened), 0)


def reply_body(pixel_total, place_ref, parts_ref, rounded_ref, notes_ref, own_ref, low_ref, *refs):
    tile_count, paired = refs[0], refs[1]
    refs = refs[2:]
    held_count = tile_count.bit_length()
    held_refs, reply_refs = refs[:held_count], refs[held_count:]
    parts = parts_ref[...]
    temporal_rounded = rounded_ref[...]
    ranks, frames = temporal_rounded.shape
    background = background_of(notes_ref, pixel_total)
    lower = (low_ref[...].astype(jnp.float32) - background).astype(jnp.bfloat16)
    pixels = 256
    bands = []
    for centered in (lower, own_ref[...]):
        sums = rows_dot(parts, centered)
        spatial = (sums[:ranks] + sums[ranks : 2 * ranks] + sums[2 * ranks :]).astype(jnp.bfloat16)
        bands += [spatial[:, q * pixels : (q + 1) * pixels] for q in range(4)]
    stacked = jnp.concatenate(bands, 0)
    place = place_ref[0]
    plane_start = place_ref[1] * tile_count
    sources = held_refs[0].shape[1]
    bits = tile_count.bit_length() - 1

    def turned(order):
        return sum(((order >> t) & 1) << (bits - 1 - t) for t in range(bits))

    def coefficients(held_ref, entry, owner):
        projected = rows_dot(stacked, held_ref[entry])
        codes = notes_ref[pl.ds(2 * (plane_start + owner) + 1, 1), :].astype(jnp.int32)
        total = jnp.zeros((ranks, sources), jnp.float32)
        for role in range(2):
            for quarter in range(4):
                start = (role * 4 + quarter) * ranks
                chosen = codes == 4 * (place - 2 * role) + quarter
                total = total + jnp.where(chosen, projected[start : start + ranks], 0.0)
        return total.astype(jnp.bfloat16)

    first = 0
    for held_ref in held_refs:
        count = held_ref.shape[0]
        if paired:
            for entry in range(count):
                offset = turned(first + entry)
                owner = lax.bitwise_xor(place, jnp.int32(offset))
                row = (offset % 2) * ranks
                reply_refs[offset // 2][row : row + ranks, :] = coefficients(held_ref, entry, owner)
        else:

            def one_owner(entry, held_ref=held_ref, first=first):
                owner = lax.bitwise_xor(place, turned(first + entry))
                reply_refs[0][owner, 0:ranks, :] = coefficients(held_ref, entry, owner)
                reply_refs[0][owner, ranks:, :] = temporal_rounded

            pl.loop(0, count)(one_owner)
        first += count
    if paired:
        for reply_ref in reply_refs:
            reply_ref[2 * ranks :, :] = temporal_rounded


def paired_trace_body(*refs):
    own_refs, mate_ref, traces_ref = refs[:-2], refs[-2], refs[-1]
    ranks = own_refs[0].shape[0] // 3
    coefficient = [r[0:ranks] for r in own_refs] + [mate_ref[i, 0:ranks] for i in range(len(own_refs))]
    temporal = [r[2 * ranks :] for r in own_refs] + [mate_ref[i, ranks:] for i in range(len(own_refs))]
    traces_ref[...] = 0.25 * columns_dot(jnp.concatenate(coefficient, 0), jnp.concatenate(temporal, 0))


def trace_body(reply_ref, traces_ref):
    owners, rows = reply_ref.shape[0], reply_ref.shape[1]
    ranks = rows // 2
    group = min(owners, 8)

    def one_group(first):
        coefficient = reply_ref[pl.ds(first, group), 0:ranks, :].reshape(group * ranks, -1)
        temporal = reply_ref[pl.ds(first, group), ranks:, :].reshape(group * ranks, -1)
        return columns_dot(coefficient, temporal)

    if owners == group:
        traces_ref[...] = 0.25 * one_group(0)
    else:
        traces_ref[...] = lax.fori_loop(
            0, owners // group, lambda i, total: total + 0.25 * one_group(i * group), jnp.zeros_like(traces_ref[...])
        )


def on_device(recording, start_vectors, footprints, source_row, footprint_block):
    tile_count = lax.axis_size("tile")
    plane_count = lax.axis_size("plane")
    devices = tile_count * plane_count
    cells, quarters, pixels, frames = recording.shape[2:]
    cell = quarters * pixels
    strip = recording.reshape(cells * cell, frames)
    start = start_vectors[0]
    patches, rank = start.shape[0], start.shape[1]
    sources = footprints.shape[1]
    pixel_total = devices * cells * cell
    f32, bf16 = jnp.float32, jnp.bfloat16

    def shape(dims, kind):
        return jax.ShapeDtypeStruct(dims, kind)

    outside = pl.BlockSpec(memory_space=pltpu.HBM)
    notes, middle, near_strip = vmem_call(
        sum_body,
        [shape((2 * devices, frames), f32), shape((cell, frames), bf16), shape(strip.shape, bf16)],
        "frame_sums",
        2 * cells * cell * frames,
        2 * cells * cell * frames,
        in_specs=[outside] * 3,
        scratch=[
            pltpu.VMEM((8, sources), jnp.int32),
            pltpu.SemaphoreType.DMA((cells,)),
            pltpu.SemaphoreType.DMA((2,)),
        ],
    )(
        *(
            pltpu.with_memory_space_constraint(x, pltpu.HBM)
            for x in (strip, source_row.reshape(1, sources), footprint_block.reshape(1, sources))
        )
    )
    notes = lax.all_to_all(notes, ("plane", "tile"), 0, 0, tiled=True)
    low_middle = from_behind(middle, "tile", -2)
    own_gram, own_middle = vmem_call(
        lambda *refs: gram_body(pixel_total, *refs),
        [shape((patches, frames, frames), f32), shape((cell, frames), bf16)],
        "own_grams",
        2 * cells * cell * frames * frames,
        2 * cells * cell * frames,
    )(notes, near_strip)
    held = [footprints]
    for bit in reversed(range(tile_count.bit_length() - 1)):
        route = [(i, i ^ (1 << bit)) for i in range(tile_count)]
        everything = held[0] if len(held) == 1 else jnp.concatenate(held, 0)
        held.append(lax.ppermute(everything, "tile", route))
    low_gram = from_behind(own_gram, "tile", -2)
    place = jnp.stack([lax.axis_index("tile"), lax.axis_index("plane")]).astype(jnp.int32)
    whole = pl.BlockSpec(memory_space=pltpu.VMEM)
    ranks = patches * rank
    temporal, parts, rounded = vmem_call(
        patch_body,
        [shape((patches, rank, frames), f32), shape((3 * ranks, frames), bf16), shape((ranks, frames), bf16)],
        "patch_factors",
        6 * 10**9,
        1 << 20,
    )(own_gram, low_gram, start)
    chips = tile_count // 2
    paired = chips <= 4
    replies = vmem_call(
        lambda *refs: reply_body(pixel_total, *refs[:6], tile_count, paired, *refs[6:]),
        [shape((3 * ranks, sources), bf16)] * chips if paired else [shape((tile_count, 2 * ranks, sources), bf16)],
        "coefficients",
        2 * 1024 * 512 * 256,
        2 << 20,
        in_specs=[pl.BlockSpec(memory_space=pltpu.SMEM)] + [whole] * (5 + len(held)),
        limit=None if paired else 40 << 20,
    )(place, parts, rounded, notes, own_middle, low_middle, *held)
    flops = 2 * sources * frames * ranks * tile_count
    if paired:
        arrived = [replies[0]]
        for offset in range(1, chips):
            route = [(i, i ^ (2 * offset)) for i in range(tile_count)]
            arrived.append(lax.ppermute(replies[offset], "tile", route))
        handed = jnp.stack([block[ranks:] for block in arrived])
        mate = lax.ppermute(handed, "tile", [(i, i ^ 1) for i in range(tile_count)])
        traces = vmem_call(
            paired_trace_body, shape((sources, frames), f32), "source_traces", flops, 1 << 19
        )(*arrived, mate)
    else:
        answers = lax.all_to_all(replies[0], "tile", 0, 0, tiled=True)
        traces = vmem_call(trace_body, shape((sources, frames), f32), "source_traces", flops, 2 * answers.size)(answers)
    return (temporal[None], traces[None])


def solution(mesh):
    placed = (
        P("plane", "tile", None, None, None, None),
        P("plane", "tile", None, None),
        P("plane", "tile", None),
        P("plane", "tile", None),
        P("plane", "tile"),
    )
    return jax.shard_map(
        on_device,
        mesh=mesh,
        in_specs=placed,
        out_specs=(P("plane", "tile", None, None), P("plane", "tile", None)),
        check_vma=False,
    )
```

```python
import jax
import jax.numpy as jnp
from jax import lax
from jax.experimental import pallas as pl
from jax.experimental.pallas import tpu as pltpu
from jax.sharding import PartitionSpec as P

ITERS = 3


def from_behind(block, axis, distance):
    devices = range(lax.axis_size(axis))
    route = [(i - distance, i) for i in devices if i - distance in devices]
    return lax.ppermute(block, axis, route)


def vmem_call(body, outs, name, flops, nbytes, in_specs=None, limit=None, scratch=()):
    params = pltpu.CompilerParams(vmem_limit_bytes=12 << 20) if limit is None else pltpu.CompilerParams(vmem_limit_bytes=limit)
    extra = {} if in_specs is None else {"in_specs": in_specs}
    return pl.pallas_call(
        body,
        out_shape=outs,
        name=name,
        compiler_params=params,
        scratch_shapes=scratch,
        cost_estimate=pl.CostEstimate(flops=flops, bytes_accessed=nbytes, transcendentals=0),
        **extra,
    )


def rows_dot(left, right):
    return lax.dot_general(left, right, (((1,), (1,)), ((), ())), preferred_element_type=jnp.float32)


def columns_dot(left, right):
    return lax.dot_general(left, right, (((0,), (0,)), ((), ())), preferred_element_type=jnp.float32)


def sum_body(strip_ref, row_ref, block_ref, notes_ref, middle_ref, held_ref, codes_ref, strip_sems, code_sems):
    cell = middle_ref.shape[0]
    cells = strip_ref.shape[0] // cell
    copies = [
        pltpu.make_async_copy(
            strip_ref.at[pl.ds(i * cell, cell)], held_ref.at[pl.ds(i * cell, cell)], strip_sems.at[i]
        )
        for i in range(cells)
    ]
    code_copies = [
        pltpu.make_async_copy(source, codes_ref.at[pl.ds(i, 1)], code_sems.at[i])
        for i, source in enumerate((row_ref, block_ref))
    ]
    for copy in copies + code_copies:
        copy.start()
    ones = jnp.ones((8, cell), jnp.bfloat16)
    total = jnp.zeros((8, strip_ref.shape[1]), jnp.float32)
    for i in range(cells):
        copies[i].wait()
        piece = held_ref[i * cell : (i + 1) * cell, :]
        total = total + jnp.dot(ones, piece, preferred_element_type=jnp.float32)
        if i == 1:
            middle_ref[...] = piece
    for copy in code_copies:
        copy.wait()
    codes = (codes_ref[0:1, :] * 4 + codes_ref[1:2, :]).astype(jnp.float32)
    odd = lax.broadcasted_iota(jnp.int32, notes_ref.shape, 0) % 2 == 1
    notes_ref[...] = jnp.where(odd, codes, total[0:1])


def background_of(notes_ref, pixel_total):
    notes = notes_ref[...]
    even = lax.broadcasted_iota(jnp.int32, notes.shape, 0) % 2 == 0
    return jnp.sum(jnp.where(even, notes, 0.0), axis=0, keepdims=True) / pixel_total


def gram_body(pixel_total, notes_ref, strip_ref, gram_ref, middle_ref):
    background = background_of(notes_ref, pixel_total)
    cell = middle_ref.shape[0]
    cells = strip_ref.shape[0] // cell
    grams = []
    for index in range(cells):
        raw = strip_ref[index * cell : (index + 1) * cell, :].astype(jnp.float32)
        centered = (raw - background).astype(jnp.bfloat16)
        if index == 1:
            middle_ref[...] = centered
        grams.append(columns_dot(centered, centered))
    for column in range(cells - 1):
        gram_ref[column] = grams[column] + grams[column + 1]


def forward_solve(grams, sides, band=16):
    rank = grams[0].shape[0]
    blocks = rank // 8
    width = 128
    sub = lax.broadcasted_iota(jnp.int32, (8, width), 0)
    pad = jnp.zeros((rank, width - rank), jnp.float32)

    def split(matrix):
        return [matrix[8 * b : 8 * b + 8] for b in range(blocks)]

    def spread(row_or_column):
        return jnp.broadcast_to(row_or_column, (8, width))

    grams = [split(jnp.concatenate([gram, pad], 1)) for gram in grams]
    sides = [[split(side) for side in group] for group in sides]
    inverse = [[None] * blocks for _ in grams]
    for start in range(0, rank, band):
        columns = [
            {
                (j, b): spread(gram[b][:, start + j : start + j + 1])
                for j in range(band)
                for b in range((start + j) // 8, blocks)
            }
            for gram in grams
        ]
        for j in range(band):
            block, line = divmod(start + j, 8)
            for patch in range(len(grams)):
                column, gram = columns[patch], grams[patch]
                pivot = 1.0 / spread(column[(j, block)][line : line + 1, :])
                known = inverse[patch][block]
                inverse[patch][block] = pivot if known is None else jnp.where(sub == line, pivot, known)
                factor = {b: column[(j, b)] * pivot for b in range(block, blocks)}
                factor[block] = jnp.where(sub > line, factor[block], 0.0)
                for later in range(j + 1, band):
                    later_block, later_line = divmod(start + later, 8)
                    entry = spread(column[(j, later_block)][later_line : later_line + 1, :])
                    for b in range(later_block, blocks):
                        column[(later, b)] = column[(later, b)] - factor[b] * entry
                targets = sides[patch] if start + band == rank else [gram] + sides[patch]
                for target in targets:
                    row = spread(target[block][line : line + 1, :])
                    for b in range(block, blocks):
                        target[b] = target[b] - factor[b] * row
    return [
        [
            jnp.concatenate([m * lax.sqrt(d) for m, d in zip(side, inverse[patch])], 0)
            for side in group
        ]
        for patch, group in enumerate(sides)
    ]


def three_parts(value):
    high = value.astype(jnp.bfloat16)
    rest = value - high.astype(jnp.float32)
    middle = rest.astype(jnp.bfloat16)
    low = (rest - middle.astype(jnp.float32)).astype(jnp.bfloat16)
    return [high, middle, low]


def patch_body(own_gram_ref, low_gram_ref, start_ref, temporal_ref, parts_ref, rounded_ref):
    patches = start_ref.shape[0]
    grams = [
        jnp.concatenate(three_parts(own_gram_ref[p] + low_gram_ref[p]), 1) for p in range(patches)
    ]
    rank, frames = start_ref.shape[1], start_ref.shape[2]
    temporal = [start_ref[p] for p in range(patches)]
    whitened = None
    for step in range(ITERS):
        rounded = [t.astype(jnp.bfloat16) for t in temporal]
        moved, inner = [], []
        for narrow, gram in zip(rounded, grams):
            terms = jnp.dot(narrow, gram, preferred_element_type=jnp.float32)
            image = terms[:, :frames] + terms[:, frames : 2 * frames] + terms[:, 2 * frames :]
            terms = rows_dot(jnp.concatenate(three_parts(image), 0), narrow)
            moved.append(image)
            inner.append(terms[:rank] + terms[rank : 2 * rank] + terms[2 * rank :])
        last = step == ITERS - 1
        sides = [[m, t.astype(jnp.float32)] if last else [m] for m, t in zip(moved, rounded)]
        solved = forward_solve(inner, sides)
        temporal = [s[0] for s in solved]
        if last:
            whitened = jnp.concatenate([s[1] for s in solved], 0)
    for p in range(patches):
        temporal_ref[p] = temporal[p]
    rounded_ref[...] = jnp.concatenate(temporal, 0).astype(jnp.bfloat16)
    parts_ref[...] = jnp.concatenate(three_parts(whitened)[:2], 0)


def reply_body(pixel_total, place_ref, parts_ref, rounded_ref, notes_ref, own_ref, low_ref, *refs):
    tile_count, paired = refs[0], refs[1]
    refs = refs[2:]
    held_count = tile_count.bit_length()
    held_refs, reply_refs = refs[:held_count], refs[held_count:]
    parts = parts_ref[...]
    temporal_rounded = rounded_ref[...]
    ranks, frames = temporal_rounded.shape
    background = background_of(notes_ref, pixel_total)
    lower = (low_ref[...].astype(jnp.float32) - background).astype(jnp.bfloat16)
    pixels = 256
    bands = []
    for centered in (lower, own_ref[...]):
        sums = rows_dot(parts, centered)
        spatial = (sums[:ranks] + sums[ranks:]).astype(jnp.bfloat16)
        bands += [spatial[:, q * pixels : (q + 1) * pixels] for q in range(4)]
    stacked = jnp.concatenate(bands, 0)
    place = place_ref[0]
    plane_start = place_ref[1] * tile_count
    sources = held_refs[0].shape[1]
    bits = tile_count.bit_length() - 1

    def turned(order):
        return sum(((order >> t) & 1) << (bits - 1 - t) for t in range(bits))

    def coefficients(weights, owners):
        projected = rows_dot(stacked, weights)
        codes = jnp.concatenate(
            [notes_ref[pl.ds(2 * (plane_start + owner) + 1, 1), :] for owner in owners], 1
        ).astype(jnp.int32)
        total = jnp.zeros((ranks, codes.shape[1]), jnp.float32)
        for role in range(2):
            for quarter in range(4):
                start = (role * 4 + quarter) * ranks
                chosen = codes == 4 * (place - 2 * role) + quarter
                total = total + jnp.where(chosen, projected[start : start + ranks], 0.0)
        return total.astype(jnp.bfloat16)

    if paired:
        listed = [(held_ref, entry) for held_ref in held_refs for entry in range(held_ref.shape[0])]
        for first in range(0, tile_count, 2):
            offsets = [turned(first), turned(first + 1)]
            weights = jnp.concatenate([held_ref[entry] for held_ref, entry in listed[first : first + 2]], 0)
            found = coefficients(weights, [lax.bitwise_xor(place, jnp.int32(offset)) for offset in offsets])
            for i, offset in enumerate(offsets):
                row = (offset % 2) * ranks
                reply_refs[offset // 2][row : row + ranks, :] = found[:, i * sources : (i + 1) * sources]
    else:
        first = 0
        for held_ref in held_refs:

            def one_owner(entry, held_ref=held_ref, first=first):
                owner = lax.bitwise_xor(place, turned(first + entry))
                reply_refs[0][owner, 0:ranks, :] = coefficients(held_ref[entry], [owner])
                reply_refs[0][owner, ranks:, :] = temporal_rounded

            pl.loop(0, held_ref.shape[0])(one_owner)
            first += held_ref.shape[0]
    if paired:
        for reply_ref in reply_refs:
            reply_ref[2 * ranks :, :] = temporal_rounded


def paired_trace_body(*refs):
    own_refs, mate_ref, traces_ref = refs[:-2], refs[-2], refs[-1]
    ranks = own_refs[0].shape[0] // 3
    coefficient = [r[0:ranks] for r in own_refs] + [mate_ref[i, 0:ranks] for i in range(len(own_refs))]
    temporal = [r[2 * ranks :] for r in own_refs] + [mate_ref[i, ranks:] for i in range(len(own_refs))]
    traces_ref[...] = 0.25 * columns_dot(jnp.concatenate(coefficient, 0), jnp.concatenate(temporal, 0))


def trace_body(reply_ref, traces_ref):
    owners, rows = reply_ref.shape[0], reply_ref.shape[1]
    ranks = rows // 2
    group = min(owners, 8)

    def one_group(first):
        coefficient = reply_ref[pl.ds(first, group), 0:ranks, :].reshape(group * ranks, -1)
        temporal = reply_ref[pl.ds(first, group), ranks:, :].reshape(group * ranks, -1)
        return columns_dot(coefficient, temporal)

    if owners == group:
        traces_ref[...] = 0.25 * one_group(0)
    else:
        traces_ref[...] = lax.fori_loop(
            0, owners // group, lambda i, total: total + 0.25 * one_group(i * group), jnp.zeros_like(traces_ref[...])
        )


def on_device(recording, start_vectors, footprints, source_row, footprint_block):
    tile_count = lax.axis_size("tile")
    plane_count = lax.axis_size("plane")
    devices = tile_count * plane_count
    cells, quarters, pixels, frames = recording.shape[2:]
    cell = quarters * pixels
    strip = recording.reshape(cells * cell, frames)
    start = start_vectors[0]
    patches, rank = start.shape[0], start.shape[1]
    sources = footprints.shape[1]
    pixel_total = devices * cells * cell
    f32, bf16 = jnp.float32, jnp.bfloat16

    def shape(dims, kind):
        return jax.ShapeDtypeStruct(dims, kind)

    outside = pl.BlockSpec(memory_space=pltpu.HBM)
    notes, middle, near_strip = vmem_call(
        sum_body,
        [shape((2 * devices, frames), f32), shape((cell, frames), bf16), shape(strip.shape, bf16)],
        "frame_sums",
        2 * cells * cell * frames,
        2 * cells * cell * frames,
        in_specs=[outside] * 3,
        scratch=[
            pltpu.VMEM((8, sources), jnp.int32),
            pltpu.SemaphoreType.DMA((cells,)),
            pltpu.SemaphoreType.DMA((2,)),
        ],
    )(
        *(
            pltpu.with_memory_space_constraint(x, pltpu.HBM)
            for x in (strip, source_row.reshape(1, sources), footprint_block.reshape(1, sources))
        )
    )
    notes = lax.all_to_all(notes, ("plane", "tile"), 0, 0, tiled=True)
    low_middle = from_behind(middle, "tile", -2)
    own_gram, own_middle = vmem_call(
        lambda *refs: gram_body(pixel_total, *refs),
        [shape((patches, frames, frames), f32), shape((cell, frames), bf16)],
        "own_grams",
        2 * cells * cell * frames * frames,
        2 * cells * cell * frames,
    )(notes, near_strip)
    held = [footprints]
    for bit in reversed(range(tile_count.bit_length() - 1)):
        route = [(i, i ^ (1 << bit)) for i in range(tile_count)]
        everything = held[0] if len(held) == 1 else jnp.concatenate(held, 0)
        held.append(lax.ppermute(everything, "tile", route))
    low_gram = from_behind(own_gram, "tile", -2)
    place = jnp.stack([lax.axis_index("tile"), lax.axis_index("plane")]).astype(jnp.int32)
    whole = pl.BlockSpec(memory_space=pltpu.VMEM)
    ranks = patches * rank
    temporal, parts, rounded = vmem_call(
        patch_body,
        [shape((patches, rank, frames), f32), shape((2 * ranks, frames), bf16), shape((ranks, frames), bf16)],
        "patch_factors",
        6 * 10**9,
        1 << 20,
    )(own_gram, low_gram, start)
    chips = tile_count // 2
    paired = chips <= 4
    replies = vmem_call(
        lambda *refs: reply_body(pixel_total, *refs[:6], tile_count, paired, *refs[6:]),
        [shape((3 * ranks, sources), bf16)] * chips if paired else [shape((tile_count, 2 * ranks, sources), bf16)],
        "coefficients",
        2 * 1024 * 512 * 256,
        2 << 20,
        in_specs=[pl.BlockSpec(memory_space=pltpu.SMEM)] + [whole] * (5 + len(held)),
        limit=None if paired else 40 << 20,
    )(place, parts, rounded, notes, own_middle, low_middle, *held)
    flops = 2 * sources * frames * ranks * tile_count
    if paired:
        arrived = [replies[0]]
        for offset in range(1, chips):
            route = [(i, i ^ (2 * offset)) for i in range(tile_count)]
            arrived.append(lax.ppermute(replies[offset], "tile", route))
        handed = jnp.stack([block[ranks:] for block in arrived])
        mate = lax.ppermute(handed, "tile", [(i, i ^ 1) for i in range(tile_count)])
        traces = vmem_call(
            paired_trace_body, shape((sources, frames), f32), "source_traces", flops, 1 << 19
        )(*arrived, mate)
    else:
        answers = lax.all_to_all(replies[0], "tile", 0, 0, tiled=True)
        traces = vmem_call(trace_body, shape((sources, frames), f32), "source_traces", flops, 2 * answers.size)(answers)
    return (temporal[None], traces[None])


def solution(mesh):
    placed = (
        P("plane", "tile", None, None, None, None),
        P("plane", "tile", None, None),
        P("plane", "tile", None),
        P("plane", "tile", None),
        P("plane", "tile"),
    )
    return jax.shard_map(
        on_device,
        mesh=mesh,
        in_specs=placed,
        out_specs=(P("plane", "tile", None, None), P("plane", "tile", None)),
        check_vma=False,
    )
```

```python
import jax
import jax.numpy as jnp
from jax import lax
from jax.experimental import pallas as pl
from jax.experimental.pallas import tpu as pltpu
from jax.sharding import PartitionSpec as P

ITERS = 3


def from_behind(block, axis, distance):
    devices = range(lax.axis_size(axis))
    route = [(i - distance, i) for i in devices if i - distance in devices]
    return lax.ppermute(block, axis, route)


def vmem_call(body, outs, name, flops, nbytes, in_specs=None, limit=None, scratch=()):
    params = pltpu.CompilerParams(vmem_limit_bytes=12 << 20) if limit is None else pltpu.CompilerParams(vmem_limit_bytes=limit)
    extra = {} if in_specs is None else {"in_specs": in_specs}
    return pl.pallas_call(
        body,
        out_shape=outs,
        name=name,
        compiler_params=params,
        scratch_shapes=scratch,
        cost_estimate=pl.CostEstimate(flops=flops, bytes_accessed=nbytes, transcendentals=0),
        **extra,
    )


def rows_dot(left, right):
    return lax.dot_general(left, right, (((1,), (1,)), ((), ())), preferred_element_type=jnp.float32)


def columns_dot(left, right):
    return lax.dot_general(left, right, (((0,), (0,)), ((), ())), preferred_element_type=jnp.float32)


def sum_body(strip_ref, row_ref, block_ref, notes_ref, middle_ref, held_ref, codes_ref, strip_sems, code_sems):
    cell = middle_ref.shape[0]
    cells = strip_ref.shape[0] // cell
    copies = [
        pltpu.make_async_copy(
            strip_ref.at[pl.ds(i * cell, cell)], held_ref.at[pl.ds(i * cell, cell)], strip_sems.at[i]
        )
        for i in range(cells)
    ]
    code_copies = [
        pltpu.make_async_copy(source, codes_ref.at[pl.ds(i, 1)], code_sems.at[i])
        for i, source in enumerate((row_ref, block_ref))
    ]
    for copy in copies + code_copies:
        copy.start()
    ones = jnp.ones((8, cell), jnp.bfloat16)
    total = jnp.zeros((8, strip_ref.shape[1]), jnp.float32)
    for i in range(cells):
        copies[i].wait()
        piece = held_ref[i * cell : (i + 1) * cell, :]
        total = total + jnp.dot(ones, piece, preferred_element_type=jnp.float32)
        if i == 1:
            middle_ref[...] = piece
    for copy in code_copies:
        copy.wait()
    codes = (codes_ref[0:1, :] * 4 + codes_ref[1:2, :]).astype(jnp.float32)
    odd = lax.broadcasted_iota(jnp.int32, notes_ref.shape, 0) % 2 == 1
    notes_ref[...] = jnp.where(odd, codes, total[0:1])


def background_of(notes_ref, pixel_total):
    notes = notes_ref[...]
    even = lax.broadcasted_iota(jnp.int32, notes.shape, 0) % 2 == 0
    return jnp.sum(jnp.where(even, notes, 0.0), axis=0, keepdims=True) / pixel_total


def gram_body(pixel_total, notes_ref, strip_ref, gram_ref, middle_ref):
    background = background_of(notes_ref, pixel_total)
    cell = middle_ref.shape[0]
    cells = strip_ref.shape[0] // cell
    grams = []
    for index in range(cells):
        raw = strip_ref[index * cell : (index + 1) * cell, :].astype(jnp.float32)
        centered = (raw - background).astype(jnp.bfloat16)
        if index == 1:
            middle_ref[...] = centered
        grams.append(columns_dot(centered, centered))
    for column in range(cells - 1):
        gram_ref[column] = grams[column] + grams[column + 1]


def forward_solve(grams, sides, band=16):
    rank = grams[0].shape[0]
    blocks = rank // 8
    width = 128
    sub = lax.broadcasted_iota(jnp.int32, (8, width), 0)
    pad = jnp.zeros((rank, width - rank), jnp.float32)

    def split(matrix):
        return [matrix[8 * b : 8 * b + 8] for b in range(blocks)]

    def spread(row_or_column):
        return jnp.broadcast_to(row_or_column, (8, width))

    grams = [split(jnp.concatenate([gram, pad], 1)) for gram in grams]
    sides = [[split(side) for side in group] for group in sides]
    inverse = [[None] * blocks for _ in grams]
    for start in range(0, rank, band):
        columns = [
            {
                (j, b): spread(gram[b][:, start + j : start + j + 1])
                for j in range(band)
                for b in range((start + j) // 8, blocks)
            }
            for gram in grams
        ]
        for j in range(band):
            block, line = divmod(start + j, 8)
            for patch in range(len(grams)):
                column, gram = columns[patch], grams[patch]
                pivot = 1.0 / spread(column[(j, block)][line : line + 1, :])
                known = inverse[patch][block]
                inverse[patch][block] = pivot if known is None else jnp.where(sub == line, pivot, known)
                factor = {b: column[(j, b)] * pivot for b in range(block, blocks)}
                factor[block] = jnp.where(sub > line, factor[block], 0.0)
                for later in range(j + 1, band):
                    later_block, later_line = divmod(start + later, 8)
                    entry = spread(column[(j, later_block)][later_line : later_line + 1, :])
                    for b in range(later_block, blocks):
                        column[(later, b)] = column[(later, b)] - factor[b] * entry
                targets = sides[patch] if start + band == rank else [gram] + sides[patch]
                for target in targets:
                    row = spread(target[block][line : line + 1, :])
                    for b in range(block, blocks):
                        target[b] = target[b] - factor[b] * row
    return [
        [
            jnp.concatenate([m * lax.sqrt(d) for m, d in zip(side, inverse[patch])], 0)
            for side in group
        ]
        for patch, group in enumerate(sides)
    ]


def three_parts(value):
    high = value.astype(jnp.bfloat16)
    rest = value - high.astype(jnp.float32)
    middle = rest.astype(jnp.bfloat16)
    low = (rest - middle.astype(jnp.float32)).astype(jnp.bfloat16)
    return [high, middle, low]


def patch_body(own_gram_ref, low_gram_ref, start_ref, temporal_ref, parts_ref, rounded_ref):
    patches = start_ref.shape[0]
    grams = [
        jnp.concatenate(three_parts(own_gram_ref[p] + low_gram_ref[p]), 1) for p in range(patches)
    ]
    rank, frames = start_ref.shape[1], start_ref.shape[2]
    temporal = [start_ref[p] for p in range(patches)]
    whitened = None
    for step in range(ITERS):
        rounded = [t.astype(jnp.bfloat16) for t in temporal]
        moved, inner = [], []
        for narrow, gram in zip(rounded, grams):
            terms = jnp.dot(narrow, gram, preferred_element_type=jnp.float32)
            image = terms[:, :frames] + terms[:, frames : 2 * frames] + terms[:, 2 * frames :]
            terms = rows_dot(jnp.concatenate(three_parts(image), 0), narrow)
            moved.append(image)
            inner.append(terms[:rank] + terms[rank : 2 * rank] + terms[2 * rank :])
        last = step == ITERS - 1
        sides = [[m, t.astype(jnp.float32)] if last else [m] for m, t in zip(moved, rounded)]
        solved = forward_solve(inner, sides)
        temporal = [s[0] for s in solved]
        if last:
            whitened = jnp.concatenate([s[1] for s in solved], 0)
    for p in range(patches):
        temporal_ref[p] = temporal[p]
    rounded_ref[...] = jnp.concatenate(temporal, 0).astype(jnp.bfloat16)
    parts_ref[...] = jnp.concatenate(three_parts(whitened)[:2], 0)


def reply_body(pixel_total, place_ref, parts_ref, rounded_ref, notes_ref, own_ref, low_ref, *refs):
    tile_count, paired = refs[0], refs[1]
    refs = refs[2:]
    held_count = tile_count.bit_length()
    held_refs, reply_refs = refs[:held_count], refs[held_count:]
    parts = parts_ref[...]
    temporal_rounded = rounded_ref[...]
    ranks, frames = temporal_rounded.shape
    background = background_of(notes_ref, pixel_total)
    lower = (low_ref[...].astype(jnp.float32) - background).astype(jnp.bfloat16)
    pixels = 256
    bands = []
    for centered in (lower, own_ref[...]):
        sums = rows_dot(parts, centered)
        spatial = (sums[:ranks] + sums[ranks:]).astype(jnp.bfloat16)
        bands += [spatial[:, q * pixels : (q + 1) * pixels] for q in range(4)]
    stacked = jnp.concatenate(bands, 0)
    place = place_ref[0]
    plane_start = place_ref[1] * tile_count
    sources = held_refs[0].shape[1]
    bits = tile_count.bit_length() - 1

    def turned(order):
        return sum(((order >> t) & 1) << (bits - 1 - t) for t in range(bits))

    def coefficients(weights, owners):
        projected = rows_dot(stacked, weights)
        codes = jnp.concatenate(
            [notes_ref[pl.ds(2 * (plane_start + owner) + 1, 1), :] for owner in owners], 1
        ).astype(jnp.int32)
        total = jnp.zeros((ranks, codes.shape[1]), jnp.float32)
        for role in range(2):
            for quarter in range(4):
                start = (role * 4 + quarter) * ranks
                chosen = codes == 4 * (place - 2 * role) + quarter
                total = total + jnp.where(chosen, projected[start : start + ranks], 0.0)
        return total.astype(jnp.bfloat16)

    if paired:
        listed = [(held_ref, entry) for held_ref in held_refs for entry in range(held_ref.shape[0])]
        for first in range(0, tile_count, 2):
            offsets = [turned(first), turned(first + 1)]
            weights = jnp.concatenate([held_ref[entry] for held_ref, entry in listed[first : first + 2]], 0)
            found = coefficients(weights, [lax.bitwise_xor(place, jnp.int32(offset)) for offset in offsets])
            for i, offset in enumerate(offsets):
                row = (offset % 2) * ranks
                reply_refs[offset // 2][row : row + ranks, :] = found[:, i * sources : (i + 1) * sources]
    else:
        first = 0
        for held_ref in held_refs:

            def one_owner(entry, held_ref=held_ref, first=first):
                owner = lax.bitwise_xor(place, turned(first + entry))
                reply_refs[0][owner, 0:ranks, :] = coefficients(held_ref[entry], [owner])
                reply_refs[0][owner, ranks:, :] = temporal_rounded

            pl.loop(0, held_ref.shape[0])(one_owner)
            first += held_ref.shape[0]
    if paired:
        for reply_ref in reply_refs:
            reply_ref[2 * ranks :, :] = temporal_rounded


def paired_trace_body(near_temporal_ref, *refs):
    own_refs, mate_ref, temporal_ref, traces_ref = refs[:-3], refs[-3], refs[-2], refs[-1]
    temporal_ref[...] = near_temporal_ref[...]
    ranks = own_refs[0].shape[0] // 3
    coefficient = [r[0:ranks] for r in own_refs] + [mate_ref[i, 0:ranks] for i in range(len(own_refs))]
    temporal = [r[2 * ranks :] for r in own_refs] + [mate_ref[i, ranks:] for i in range(len(own_refs))]
    traces_ref[...] = 0.25 * columns_dot(jnp.concatenate(coefficient, 0), jnp.concatenate(temporal, 0))


def trace_body(reply_ref, traces_ref):
    owners, rows = reply_ref.shape[0], reply_ref.shape[1]
    ranks = rows // 2
    group = min(owners, 8)

    def one_group(first):
        coefficient = reply_ref[pl.ds(first, group), 0:ranks, :].reshape(group * ranks, -1)
        temporal = reply_ref[pl.ds(first, group), ranks:, :].reshape(group * ranks, -1)
        return columns_dot(coefficient, temporal)

    if owners == group:
        traces_ref[...] = 0.25 * one_group(0)
    else:
        traces_ref[...] = lax.fori_loop(
            0, owners // group, lambda i, total: total + 0.25 * one_group(i * group), jnp.zeros_like(traces_ref[...])
        )


def on_device(recording, start_vectors, footprints, source_row, footprint_block):
    tile_count = lax.axis_size("tile")
    plane_count = lax.axis_size("plane")
    devices = tile_count * plane_count
    cells, quarters, pixels, frames = recording.shape[2:]
    cell = quarters * pixels
    strip = recording.reshape(cells * cell, frames)
    start = start_vectors[0]
    patches, rank = start.shape[0], start.shape[1]
    sources = footprints.shape[1]
    pixel_total = devices * cells * cell
    f32, bf16 = jnp.float32, jnp.bfloat16

    def shape(dims, kind):
        return jax.ShapeDtypeStruct(dims, kind)

    outside = pl.BlockSpec(memory_space=pltpu.HBM)
    notes, middle, near_strip = vmem_call(
        sum_body,
        [shape((2 * devices, frames), f32), shape((cell, frames), bf16), shape(strip.shape, bf16)],
        "frame_sums",
        2 * cells * cell * frames,
        2 * cells * cell * frames,
        in_specs=[outside] * 3,
        scratch=[
            pltpu.VMEM((8, sources), jnp.int32),
            pltpu.SemaphoreType.DMA((cells,)),
            pltpu.SemaphoreType.DMA((2,)),
        ],
    )(
        *(
            pltpu.with_memory_space_constraint(x, pltpu.HBM)
            for x in (strip, source_row.reshape(1, sources), footprint_block.reshape(1, sources))
        )
    )
    notes = lax.all_to_all(notes, ("plane", "tile"), 0, 0, tiled=True)
    low_middle = from_behind(middle, "tile", -2)
    own_gram, own_middle = vmem_call(
        lambda *refs: gram_body(pixel_total, *refs),
        [shape((patches, frames, frames), f32), shape((cell, frames), bf16)],
        "own_grams",
        2 * cells * cell * frames * frames,
        2 * cells * cell * frames,
    )(notes, near_strip)
    held = [footprints]
    for bit in reversed(range(tile_count.bit_length() - 1)):
        route = [(i, i ^ (1 << bit)) for i in range(tile_count)]
        everything = held[0] if len(held) == 1 else jnp.concatenate(held, 0)
        held.append(lax.ppermute(everything, "tile", route))
    low_gram = from_behind(own_gram, "tile", -2)
    place = jnp.stack([lax.axis_index("tile"), lax.axis_index("plane")]).astype(jnp.int32)
    whole = pl.BlockSpec(memory_space=pltpu.VMEM)
    ranks = patches * rank
    temporal, parts, rounded = vmem_call(
        patch_body,
        [shape((patches, rank, frames), f32), shape((2 * ranks, frames), bf16), shape((ranks, frames), bf16)],
        "patch_factors",
        6 * 10**9,
        1 << 20,
    )(own_gram, low_gram, start)
    chips = tile_count // 2
    paired = chips <= 4
    replies = vmem_call(
        lambda *refs: reply_body(pixel_total, *refs[:6], tile_count, paired, *refs[6:]),
        [shape((3 * ranks, sources), bf16)] * chips if paired else [shape((tile_count, 2 * ranks, sources), bf16)],
        "coefficients",
        2 * 1024 * 512 * 256,
        2 << 20,
        in_specs=[pl.BlockSpec(memory_space=pltpu.SMEM)] + [whole] * (5 + len(held)),
        limit=None if paired else 40 << 20,
    )(place, parts, rounded, notes, own_middle, low_middle, *held)
    flops = 2 * sources * frames * ranks * tile_count
    if paired:
        arrived = [replies[0]]
        for offset in range(1, chips):
            route = [(i, i ^ (2 * offset)) for i in range(tile_count)]
            arrived.append(lax.ppermute(replies[offset], "tile", route))
        handed = jnp.stack([block[ranks:] for block in arrived])
        mate = lax.ppermute(handed, "tile", [(i, i ^ 1) for i in range(tile_count)])
        temporal, traces = vmem_call(
            paired_trace_body,
            [shape(temporal.shape, f32), shape((sources, frames), f32)],
            "source_traces",
            flops,
            1 << 19,
        )(temporal, *arrived, mate)
    else:
        answers = lax.all_to_all(replies[0], "tile", 0, 0, tiled=True)
        traces = vmem_call(trace_body, shape((sources, frames), f32), "source_traces", flops, 2 * answers.size)(answers)
    return (temporal[None], traces[None])


def solution(mesh):
    placed = (
        P("plane", "tile", None, None, None, None),
        P("plane", "tile", None, None),
        P("plane", "tile", None),
        P("plane", "tile", None),
        P("plane", "tile"),
    )
    return jax.shard_map(
        on_device,
        mesh=mesh,
        in_specs=placed,
        out_specs=(P("plane", "tile", None, None), P("plane", "tile", None)),
        check_vma=False,
    )
```

```python
import jax
import jax.numpy as jnp
from jax import lax
from jax.experimental import pallas as pl
from jax.experimental.pallas import tpu as pltpu
from jax.sharding import PartitionSpec as P

ITERS = 3


def from_behind(block, axis, distance):
    devices = range(lax.axis_size(axis))
    route = [(i - distance, i) for i in devices if i - distance in devices]
    return lax.ppermute(block, axis, route)


def vmem_call(body, outs, name, flops, nbytes, in_specs=None, limit=None, scratch=()):
    params = pltpu.CompilerParams(vmem_limit_bytes=12 << 20) if limit is None else pltpu.CompilerParams(vmem_limit_bytes=limit)
    extra = {} if in_specs is None else {"in_specs": in_specs}
    return pl.pallas_call(
        body,
        out_shape=outs,
        name=name,
        compiler_params=params,
        scratch_shapes=scratch,
        cost_estimate=pl.CostEstimate(flops=flops, bytes_accessed=nbytes, transcendentals=0),
        **extra,
    )


def rows_dot(left, right):
    return lax.dot_general(left, right, (((1,), (1,)), ((), ())), preferred_element_type=jnp.float32)


def columns_dot(left, right):
    return lax.dot_general(left, right, (((0,), (0,)), ((), ())), preferred_element_type=jnp.float32)


def sum_body(strip_ref, row_ref, block_ref, notes_ref, middle_ref, held_ref, codes_ref, strip_sems, code_sems):
    cell = middle_ref.shape[0]
    cells = strip_ref.shape[0] // cell
    copies = [
        pltpu.make_async_copy(
            strip_ref.at[pl.ds(i * cell, cell)], held_ref.at[pl.ds(i * cell, cell)], strip_sems.at[i]
        )
        for i in range(cells)
    ]
    code_copies = [
        pltpu.make_async_copy(source, codes_ref.at[pl.ds(i, 1)], code_sems.at[i])
        for i, source in enumerate((row_ref, block_ref))
    ]
    for copy in copies + code_copies:
        copy.start()
    ones = jnp.ones((8, cell), jnp.bfloat16)
    total = jnp.zeros((8, strip_ref.shape[1]), jnp.float32)
    for i in range(cells):
        copies[i].wait()
        piece = held_ref[i * cell : (i + 1) * cell, :]
        total = total + jnp.dot(ones, piece, preferred_element_type=jnp.float32)
        if i == 1:
            middle_ref[...] = piece
    for copy in code_copies:
        copy.wait()
    codes = (codes_ref[0:1, :] * 4 + codes_ref[1:2, :]).astype(jnp.float32)
    odd = lax.broadcasted_iota(jnp.int32, notes_ref.shape, 0) % 2 == 1
    notes_ref[...] = jnp.where(odd, codes, total[0:1])


def background_of(notes_ref, pixel_total):
    notes = notes_ref[...]
    even = lax.broadcasted_iota(jnp.int32, notes.shape, 0) % 2 == 0
    return jnp.sum(jnp.where(even, notes, 0.0), axis=0, keepdims=True) / pixel_total


def gram_body(pixel_total, notes_ref, strip_ref, gram_ref, middle_ref):
    background = background_of(notes_ref, pixel_total)
    cell = middle_ref.shape[0]
    cells = strip_ref.shape[0] // cell
    grams = []
    for index in range(cells):
        raw = strip_ref[index * cell : (index + 1) * cell, :].astype(jnp.float32)
        centered = (raw - background).astype(jnp.bfloat16)
        if index == 1:
            middle_ref[...] = centered
        grams.append(columns_dot(centered, centered))
    for column in range(cells - 1):
        gram_ref[column] = grams[column] + grams[column + 1]


def forward_solve(grams, sides, band=16):
    rank = grams[0].shape[0]
    blocks = rank // 8
    width = 128
    sub = lax.broadcasted_iota(jnp.int32, (8, width), 0)
    pad = jnp.zeros((rank, width - rank), jnp.float32)

    def split(matrix):
        return [matrix[8 * b : 8 * b + 8] for b in range(blocks)]

    def spread(row_or_column):
        return jnp.broadcast_to(row_or_column, (8, width))

    grams = [split(jnp.concatenate([gram, pad], 1)) for gram in grams]
    sides = [[split(side) for side in group] for group in sides]
    inverse = [[None] * blocks for _ in grams]
    for start in range(0, rank, band):
        columns = [
            {
                (j, b): spread(gram[b][:, start + j : start + j + 1])
                for j in range(band)
                for b in range((start + j) // 8, blocks)
            }
            for gram in grams
        ]
        for j in range(band):
            block, line = divmod(start + j, 8)
            for patch in range(len(grams)):
                column, gram = columns[patch], grams[patch]
                pivot = 1.0 / spread(column[(j, block)][line : line + 1, :])
                known = inverse[patch][block]
                inverse[patch][block] = pivot if known is None else jnp.where(sub == line, pivot, known)
                factor = {b: column[(j, b)] * pivot for b in range(block, blocks)}
                factor[block] = jnp.where(sub > line, factor[block], 0.0)
                for later in range(j + 1, band):
                    later_block, later_line = divmod(start + later, 8)
                    entry = spread(column[(j, later_block)][later_line : later_line + 1, :])
                    for b in range(later_block, blocks):
                        column[(later, b)] = column[(later, b)] - factor[b] * entry
                targets = sides[patch] if start + band == rank else [gram] + sides[patch]
                for target in targets:
                    row = spread(target[block][line : line + 1, :])
                    for b in range(block, blocks):
                        target[b] = target[b] - factor[b] * row
    return [
        [
            jnp.concatenate([m * lax.sqrt(d) for m, d in zip(side, inverse[patch])], 0)
            for side in group
        ]
        for patch, group in enumerate(sides)
    ]


def three_parts(value):
    high = value.astype(jnp.bfloat16)
    rest = value - high.astype(jnp.float32)
    middle = rest.astype(jnp.bfloat16)
    low = (rest - middle.astype(jnp.float32)).astype(jnp.bfloat16)
    return [high, middle, low]


def patch_body(own_gram_ref, low_gram_ref, start_ref, temporal_ref, parts_ref, rounded_ref):
    patches = start_ref.shape[0]
    grams = [
        jnp.concatenate(three_parts(own_gram_ref[p] + low_gram_ref[p]), 0) for p in range(patches)
    ]
    rank, frames = start_ref.shape[1], start_ref.shape[2]
    temporal = [start_ref[p] for p in range(patches)]
    whitened = None
    for step in range(ITERS):
        rounded = [t.astype(jnp.bfloat16) for t in temporal]
        moved, inner = [], []
        for narrow, gram in zip(rounded, grams):
            repeated = jnp.concatenate([narrow] * 3, 1)
            image = jnp.dot(repeated, gram, preferred_element_type=jnp.float32)
            terms = rows_dot(jnp.concatenate(three_parts(image), 0), narrow)
            moved.append(image)
            inner.append(terms[:rank] + terms[rank : 2 * rank] + terms[2 * rank :])
        last = step == ITERS - 1
        sides = [[m, t.astype(jnp.float32)] if last else [m] for m, t in zip(moved, rounded)]
        solved = forward_solve(inner, sides)
        temporal = [s[0] for s in solved]
        if last:
            whitened = jnp.concatenate([s[1] for s in solved], 0)
    for p in range(patches):
        temporal_ref[p] = temporal[p]
    rounded_ref[...] = jnp.concatenate(temporal, 0).astype(jnp.bfloat16)
    parts_ref[...] = jnp.concatenate(three_parts(whitened)[:2], 0)


def reply_body(pixel_total, place_ref, parts_ref, rounded_ref, notes_ref, own_ref, low_ref, *refs):
    tile_count, paired = refs[0], refs[1]
    refs = refs[2:]
    held_count = tile_count.bit_length()
    held_refs, reply_refs = refs[:held_count], refs[held_count:]
    parts = parts_ref[...]
    temporal_rounded = rounded_ref[...]
    ranks, frames = temporal_rounded.shape
    background = background_of(notes_ref, pixel_total)
    lower = (low_ref[...].astype(jnp.float32) - background).astype(jnp.bfloat16)
    pixels = 256
    bands = []
    for centered in (lower, own_ref[...]):
        sums = rows_dot(parts, centered)
        spatial = (sums[:ranks] + sums[ranks:]).astype(jnp.bfloat16)
        bands += [spatial[:, q * pixels : (q + 1) * pixels] for q in range(4)]
    stacked = jnp.concatenate(bands, 0)
    place = place_ref[0]
    plane_start = place_ref[1] * tile_count
    sources = held_refs[0].shape[1]
    bits = tile_count.bit_length() - 1

    def turned(order):
        return sum(((order >> t) & 1) << (bits - 1 - t) for t in range(bits))

    def coefficients(weights, owners):
        projected = rows_dot(stacked, weights)
        codes = jnp.concatenate(
            [notes_ref[pl.ds(2 * (plane_start + owner) + 1, 1), :] for owner in owners], 1
        ).astype(jnp.int32)
        total = jnp.zeros((ranks, codes.shape[1]), jnp.float32)
        for role in range(2):
            for quarter in range(4):
                start = (role * 4 + quarter) * ranks
                chosen = codes == 4 * (place - 2 * role) + quarter
                total = total + jnp.where(chosen, projected[start : start + ranks], 0.0)
        return total.astype(jnp.bfloat16)

    if paired:
        listed = [(held_ref, entry) for held_ref in held_refs for entry in range(held_ref.shape[0])]
        for first in range(0, tile_count, 2):
            offsets = [turned(first), turned(first + 1)]
            weights = jnp.concatenate([held_ref[entry] for held_ref, entry in listed[first : first + 2]], 0)
            found = coefficients(weights, [lax.bitwise_xor(place, jnp.int32(offset)) for offset in offsets])
            for i, offset in enumerate(offsets):
                row = (offset % 2) * ranks
                reply_refs[offset // 2][row : row + ranks, :] = found[:, i * sources : (i + 1) * sources]
    else:
        first = 0
        for held_ref in held_refs:

            def one_owner(entry, held_ref=held_ref, first=first):
                owner = lax.bitwise_xor(place, turned(first + entry))
                reply_refs[0][owner, 0:ranks, :] = coefficients(held_ref[entry], [owner])
                reply_refs[0][owner, ranks:, :] = temporal_rounded

            pl.loop(0, held_ref.shape[0])(one_owner)
            first += held_ref.shape[0]
    if paired:
        for reply_ref in reply_refs:
            reply_ref[2 * ranks :, :] = temporal_rounded


def direct_trace_body(*refs):
    own_refs, traces_ref = refs[:-1], refs[-1]
    ranks = own_refs[0].shape[0] // 3
    coefficient = jnp.concatenate([r[0:ranks] for r in own_refs], 0)
    temporal = jnp.concatenate([r[2 * ranks :] for r in own_refs], 0)
    traces_ref[...] = columns_dot(coefficient, temporal)


def mate_trace_body(near_temporal_ref, direct_ref, mate_ref, temporal_ref, traces_ref):
    temporal_ref[...] = near_temporal_ref[...]
    count, ranks = mate_ref.shape[0], mate_ref.shape[1] // 2
    coefficient = jnp.concatenate([mate_ref[i, 0:ranks] for i in range(count)], 0)
    temporal = jnp.concatenate([mate_ref[i, ranks:] for i in range(count)], 0)
    traces_ref[...] = 0.25 * (direct_ref[...] + columns_dot(coefficient, temporal))


def trace_body(reply_ref, traces_ref):
    owners, rows = reply_ref.shape[0], reply_ref.shape[1]
    ranks = rows // 2
    group = min(owners, 8)

    def one_group(first):
        coefficient = reply_ref[pl.ds(first, group), 0:ranks, :].reshape(group * ranks, -1)
        temporal = reply_ref[pl.ds(first, group), ranks:, :].reshape(group * ranks, -1)
        return columns_dot(coefficient, temporal)

    if owners == group:
        traces_ref[...] = 0.25 * one_group(0)
    else:
        traces_ref[...] = lax.fori_loop(
            0, owners // group, lambda i, total: total + 0.25 * one_group(i * group), jnp.zeros_like(traces_ref[...])
        )


def on_device(recording, start_vectors, footprints, source_row, footprint_block):
    tile_count = lax.axis_size("tile")
    plane_count = lax.axis_size("plane")
    devices = tile_count * plane_count
    cells, quarters, pixels, frames = recording.shape[2:]
    cell = quarters * pixels
    strip = recording.reshape(cells * cell, frames)
    start = start_vectors[0]
    patches, rank = start.shape[0], start.shape[1]
    sources = footprints.shape[1]
    pixel_total = devices * cells * cell
    f32, bf16 = jnp.float32, jnp.bfloat16

    def shape(dims, kind):
        return jax.ShapeDtypeStruct(dims, kind)

    outside = pl.BlockSpec(memory_space=pltpu.HBM)
    notes, middle, near_strip = vmem_call(
        sum_body,
        [shape((2 * devices, frames), f32), shape((cell, frames), bf16), shape(strip.shape, bf16)],
        "frame_sums",
        2 * cells * cell * frames,
        2 * cells * cell * frames,
        in_specs=[outside] * 3,
        scratch=[
            pltpu.VMEM((8, sources), jnp.int32),
            pltpu.SemaphoreType.DMA((cells,)),
            pltpu.SemaphoreType.DMA((2,)),
        ],
    )(
        *(
            pltpu.with_memory_space_constraint(x, pltpu.HBM)
            for x in (strip, source_row.reshape(1, sources), footprint_block.reshape(1, sources))
        )
    )
    notes = lax.all_to_all(notes, ("plane", "tile"), 0, 0, tiled=True)
    low_middle = from_behind(middle, "tile", -2)
    own_gram, own_middle = vmem_call(
        lambda *refs: gram_body(pixel_total, *refs),
        [shape((patches, frames, frames), f32), shape((cell, frames), bf16)],
        "own_grams",
        2 * cells * cell * frames * frames,
        2 * cells * cell * frames,
    )(notes, near_strip)
    held = [footprints]
    for bit in reversed(range(tile_count.bit_length() - 1)):
        route = [(i, i ^ (1 << bit)) for i in range(tile_count)]
        everything = held[0] if len(held) == 1 else jnp.concatenate(held, 0)
        held.append(lax.ppermute(everything, "tile", route))
    low_gram = from_behind(own_gram, "tile", -2)
    place = jnp.stack([lax.axis_index("tile"), lax.axis_index("plane")]).astype(jnp.int32)
    whole = pl.BlockSpec(memory_space=pltpu.VMEM)
    ranks = patches * rank
    temporal, parts, rounded = vmem_call(
        patch_body,
        [shape((patches, rank, frames), f32), shape((2 * ranks, frames), bf16), shape((ranks, frames), bf16)],
        "patch_factors",
        6 * 10**9,
        1 << 20,
    )(own_gram, low_gram, start)
    chips = tile_count // 2
    paired = chips <= 4
    replies = vmem_call(
        lambda *refs: reply_body(pixel_total, *refs[:6], tile_count, paired, *refs[6:]),
        [shape((3 * ranks, sources), bf16)] * chips if paired else [shape((tile_count, 2 * ranks, sources), bf16)],
        "coefficients",
        2 * 1024 * 512 * 256,
        2 << 20,
        in_specs=[pl.BlockSpec(memory_space=pltpu.SMEM)] + [whole] * (5 + len(held)),
        limit=None if paired else 40 << 20,
    )(place, parts, rounded, notes, own_middle, low_middle, *held)
    flops = 2 * sources * frames * ranks * tile_count
    if paired:
        arrived = [replies[0]]
        for offset in range(1, chips):
            route = [(i, i ^ (2 * offset)) for i in range(tile_count)]
            arrived.append(lax.ppermute(replies[offset], "tile", route))
        handed = jnp.stack([block[ranks:] for block in arrived])
        mate = lax.ppermute(handed, "tile", [(i, i ^ 1) for i in range(tile_count)])
        direct = vmem_call(
            direct_trace_body, shape((sources, frames), f32), "direct_traces", flops // 2, 1 << 18
        )(*arrived)
        temporal, traces = vmem_call(
            mate_trace_body,
            [shape(temporal.shape, f32), shape((sources, frames), f32)],
            "source_traces",
            flops // 2,
            1 << 18,
        )(temporal, direct, mate)
    else:
        answers = lax.all_to_all(replies[0], "tile", 0, 0, tiled=True)
        traces = vmem_call(trace_body, shape((sources, frames), f32), "source_traces", flops, 2 * answers.size)(answers)
    return (temporal[None], traces[None])


def solution(mesh):
    placed = (
        P("plane", "tile", None, None, None, None),
        P("plane", "tile", None, None),
        P("plane", "tile", None),
        P("plane", "tile", None),
        P("plane", "tile"),
    )
    return jax.shard_map(
        on_device,
        mesh=mesh,
        in_specs=placed,
        out_specs=(P("plane", "tile", None, None), P("plane", "tile", None)),
        check_vma=False,
    )
```
